256 devices in a mesh: section: 4 (over y), ctx: 16 (over z_lo, x), tp: 4 (over z_hi, core).
Axes of the slice: x: 4, y: 4, z: 8 (z_hi: 2, z_lo: 4; z = z_hi * 4 + z_lo), core: 2. Of those that a mesh axis runs over, the one named last changes fastest.
Arguments:
- query_heads: bfloat16 [4, 2, 2048, 6144], P('section', None, 'ctx', 'tp'), may hold values from -8 to 8
- keys_values: bfloat16 [4, 2048, 2, 1024], P('section', 'ctx', None, 'tp'), may hold values from -12 to 12
- grad_output: bfloat16 [4, 2, 2048, 6144], P('section', None, 'ctx', 'tp'), may hold values from -6 to 6
- norm_gain: float32 [4, 2, 6144], P('section', None, 'tp'), may hold values from 0.1 to 1.9
- turn_ids: int32 [2048], P('ctx'), may hold values from 0 to 63, never falling along the last dimension, each value on 1 to 64 neighbouring positions
Outputs:
- normed_out: bfloat16 [4, 2, 2048, 6144], P('section', None, 'ctx', 'tp')
- query_grad: bfloat16 [4, 2, 2048, 6144], P('section', None, 'ctx', 'tp')
- kv_grad: float32 [4, 2048, 2, 1024], P('section', 'ctx', None, 'tp')
The draws below stay inside these ranges and needn't reach their ends.
Inputs may be any that keep to these rules, and one draw needn't show every extreme that they name: `turn_ids`: turn numbers never fall along the dialogue; a turn holds 1 to 64 positions and one holds exactly 64; every turn number occurs.
All inputs are finite; a program needn't handle non-finite values.
Results may differ from the reference program's by a relative error of at most 0.015.
Values may be sent and summed in bfloat16 or wider, within the bound.
No kernel may reach another device: no remote copies, remote signals or barrier semaphores. Data moves between devices by JAX's collectives and lax.ppermute only.
A program may use at most 64 MiB of HBM per device.

```python
import math
import jax
import jax.numpy as jnp
import numpy as np
from jax import lax

HD = 128
KVH = 8
GROUP = 6
HQ = 48
SEQ = 2048
SECTIONS = 4
TURNS = 64
TURN_MOST = 64


def draw_query_heads(key, part):
    shape_full = (SECTIONS, 2, SEQ, KVH, GROUP, HD)
    drawn = jax.random.normal(jax.random.fold_in(key, 11), shape_full, jnp.float32)
    drawn = jnp.clip(drawn, -8.0, 8.0)
    return drawn.reshape(SECTIONS, 2, SEQ, KVH * GROUP * HD).astype(jnp.bfloat16)


def draw_keys_values(key, part):
    shape_half = (SECTIONS, SEQ, KVH, HD)
    ladder = jnp.arange(KVH, dtype=jnp.float32) / (KVH - 1)
    key_part = jax.random.normal(jax.random.fold_in(key, 21), shape_half, jnp.float32)
    value_part = jax.random.normal(jax.random.fold_in(key, 22), shape_half, jnp.float32)
    head_scale = 0.3 * 10.0 ** ladder
    value_part = value_part * head_scale[None, None, :, None]
    stacked = jnp.clip(jnp.stack([key_part, value_part], axis=2), -12.0, 12.0)
    return stacked.reshape(SECTIONS, SEQ, 2, KVH * HD).astype(jnp.bfloat16)


def steps_of(stream_key, shape, split, least, top_value):
    def one(axis_at, parts):
        steps = jax.random.uniform(jax.random.fold_in(jax.random.fold_in(stream_key, 6), axis_at), (parts,), jnp.float32, least / len(split), top_value / len(split))
        return jnp.repeat(jnp.exp(steps), shape[axis_at] // parts).reshape((-1,) + (1,) * (len(shape) - axis_at - 1))

    factor_of = one(*split[0])
    for cut in split[1:]:
        factor_of = factor_of * one(*cut)
    return factor_of


def split_up(count, total, limit, slope):
    weights = [(1 << 20) // math.isqrt(standing ** slope) + 1 for standing in range(2, count + 1)]
    surplus, holding = total - limit - (count - 1), [1] * (count - 1)
    while surplus > 0:
        movable = [i for i in range(count - 1) if holding[i] < limit]
        mass, remaining = sum([weights[i] for i in movable]), surplus
        for i in movable:
            addition = min(limit - holding[i], max(1, remaining * weights[i] // mass), surplus)
            holding[i] = holding[i] + addition
            surplus = surplus - addition
    return np.array([limit] + holding)


def ragged(stream_key, number_of, total, bound, skew):
    if number_of == 2:
        one = jax.random.randint(stream_key, (), max(1, total - bound), min(bound, total - 1) + 1)
        return jnp.stack([one, total - one])
    lengths = jnp.asarray(split_up(number_of, total, bound, skew), jnp.int32)
    pairs = (number_of - 1) // 2
    giver, sink = lengths[1:1 + 2 * pairs:2], lengths[2:2 + 2 * pairs:2]
    room = jnp.minimum(giver - 1, bound - sink)
    passed = jax.random.randint(jax.random.fold_in(stream_key, 1), (pairs,), 0, 1 << 20) % (room + 1)
    lengths = lengths.at[1:1 + 2 * pairs:2].set(giver - passed).at[2:2 + 2 * pairs:2].set(sink + passed)
    return lengths[jax.random.permutation(jax.random.fold_in(stream_key, 2), number_of)]


def centred(stream_key, shape, width, bound, cuts=(), kind=jnp.bfloat16):
    gain = steps_of(stream_key, shape, cuts, -0.22, 0.18) if cuts else 1.0
    result = jax.random.normal(stream_key, shape, jnp.float32) * width * gain
    return jnp.minimum(jnp.maximum(result, -bound), bound).astype(kind)


def setup_inputs(seed: int = 0) -> dict:
    streams_of = jax.random.split(jax.random.key(seed), 6)
    return {
        "query_heads": draw_query_heads(jax.random.fold_in(streams_of[5], 71), 0),
        "keys_values": draw_keys_values(jax.random.fold_in(streams_of[5], 71), 0),
        "grad_output": centred(streams_of[2], (SECTIONS, 2, SEQ, HQ * HD), 1.0, 6.0, ((0, 4), (2, 16), (3, 4))),
        "norm_gain": jnp.clip(1.0 + 0.18 * jax.random.normal(streams_of[3], (SECTIONS, 2, HQ * HD), jnp.float32), 0.1, 1.9),
        "turn_ids": jnp.searchsorted(jnp.cumsum(ragged(streams_of[4], TURNS, SEQ, TURN_MOST, 2)), jnp.arange(SEQ), side="right").astype(jnp.int32),
    }


neg_big = -1e+30
eps_norm = 1e-06

def round_trip(values):
    return lax.optimization_barrier(values.astype(jnp.bfloat16)).astype(jnp.float32)

def head_weights(query_head, key_head, visible):
    scores = jnp.einsum('qgd,kd->gqk', query_head.astype(jnp.float32), key_head.astype(jnp.float32)) * HD ** (-0.5)
    row_max = lax.optimization_barrier(jnp.max(jnp.where(visible, scores, neg_big), axis=-1))
    weights = jnp.where(visible, jnp.exp(scores - row_max[..., None]), 0.0)
    return (weights, lax.optimization_barrier(jnp.sum(weights, axis=-1)))

def one_layer(query_flat, kv_rows, gain_vector, cotangent_flat, turn_rows):
    positions = jnp.arange(SEQ, dtype=jnp.int32)
    visible = (positions[None, :] <= positions[:, None]) | (turn_rows[None, :] == turn_rows[:, None])
    queries = query_flat.reshape(SEQ, KVH, GROUP, HD).transpose(1, 0, 2, 3)
    key_rows = kv_rows[:, 0].reshape(SEQ, KVH, HD).transpose(1, 0, 2)
    value_rows = kv_rows[:, 1].reshape(SEQ, KVH, HD).transpose(1, 0, 2)

    def forward_head(pieces):
        query_head, key_head, value_head = pieces
        weights, totals = head_weights(query_head, key_head, visible)
        mixture = jnp.einsum('gqk,kd->qgd', round_trip(weights), value_head.astype(jnp.float32))
        return mixture / jnp.transpose(totals)[..., None]
    output = lax.map(forward_head, (queries, key_rows, value_rows))
    output = jnp.transpose(output, (1, 0, 2, 3)).reshape(SEQ, KVH * GROUP * HD)
    inverse = lax.rsqrt(lax.optimization_barrier(jnp.mean(output * output, axis=-1)) + eps_norm)
    normed = (output * inverse[:, None] * gain_vector).astype(jnp.bfloat16)
    scaled = cotangent_flat.astype(jnp.float32) * gain_vector
    center = lax.optimization_barrier(jnp.mean(scaled * output, axis=-1))
    out_grad = round_trip(inverse[:, None] * (scaled - output * (inverse * inverse * center)[:, None]))
    grad_rows = out_grad.reshape(SEQ, KVH, GROUP, HD).transpose(1, 0, 2, 3)
    out_rows = output.reshape(SEQ, KVH, GROUP, HD).transpose(1, 0, 2, 3)

    def backward_head(pieces):
        query_head, key_head, value_head, grad_head, out_head = pieces
        weights, totals = head_weights(query_head, key_head, visible)
        chances = weights / totals[..., None]
        row_dot = jnp.transpose(lax.optimization_barrier(jnp.sum(grad_head * out_head, axis=-1)))
        value_grad = jnp.einsum('gqk,qgd->kd', round_trip(chances), grad_head)
        prob_grad = jnp.einsum('qgd,kd->gqk', grad_head, value_head.astype(jnp.float32))
        score_grad = round_trip(chances * (prob_grad - row_dot[..., None]))
        query_part = jnp.einsum('gqk,kd->qgd', score_grad, key_head.astype(jnp.float32)) * HD ** (-0.5)
        key_grad = jnp.einsum('gqk,qgd->kd', score_grad, query_head.astype(jnp.float32)) * HD ** (-0.5)
        return (query_part, jnp.stack([key_grad, value_grad], axis=1))
    query_part, kv_part = lax.map(backward_head, (queries, key_rows, value_rows, grad_rows, out_rows))
    query_part = jnp.transpose(query_part, (1, 0, 2, 3)).reshape(SEQ, KVH * GROUP * HD).astype(jnp.bfloat16)
    kv_part = jnp.transpose(kv_part, (1, 2, 0, 3)).reshape(SEQ, 2, KVH * HD)
    return (normed, query_part, kv_part)

def reference(query_heads, keys_values, grad_output, norm_gain, turn_ids):
    normed_all = []
    qgrad_all = []
    produced = []
    consumed = []
    for section_index in range(SECTIONS):
        producer = one_layer(query_heads[section_index, 0], keys_values[section_index], norm_gain[section_index, 0], grad_output[section_index, 0], turn_ids)
        consumer = one_layer(query_heads[section_index, 1], keys_values[(section_index - 1) % SECTIONS], norm_gain[section_index, 1], grad_output[section_index, 1], turn_ids)
        normed_all.append(jnp.stack([producer[0], consumer[0]]))
        qgrad_all.append(jnp.stack([producer[1], consumer[1]]))
        produced.append(producer[2])
        consumed.append(consumer[2])
    kv_grad = jnp.stack([produced[section_index] + consumed[(section_index + 1) % SECTIONS] for section_index in range(SECTIONS)])
    return (jnp.stack(normed_all), jnp.stack(qgrad_all), kv_grad)
```

```python
import math

import jax
import jax.numpy as jnp
from jax import lax
from jax.experimental import pallas as pl
from jax.experimental.pallas import tpu as pltpu
from jax.sharding import Mesh
from jax.sharding import PartitionSpec as P

HD = 128
KVH = 8
GROUP = 6
FEATURES = KVH * GROUP * HD
CTX = ("ctx_0", "ctx_1")
OWN, HALO, PAST = 512, 128, 512
WIDTH = OWN + HALO + 3 * PAST
SCALE = HD**-0.5
SCALE_LOG2 = SCALE * math.log2(math.e)

neg_big = -1e30
eps_norm = 1e-06
bf16 = jnp.bfloat16
f32 = jnp.float32


def dot_nt(a, b):
    return lax.dot_general(a, b, (((1,), (1,)), ((), ())), preferred_element_type=f32)


def dot_nn(a, b):
    return lax.dot_general(a, b, (((1,), (0,)), ((), ())), preferred_element_type=f32)


def slot(x, d):
    return pl.ds(pl.multiple_of(((x - d) & 3) * 128, 128), 128)


def column_of(row):
    return jnp.transpose(jnp.broadcast_to(row, (128, 128)))


def order_kernel(info, a0, a1, a2, a3, own, first, turns):
    x = info[0]
    for d, ref in enumerate((a0, a1, a2, a3)):
        rows = slot(x, d)
        own[0, rows, :] = ref[0:128, :]
        own[1, rows, :] = ref[128:256, :]
        at = (x - d) & 3
        turns[pl.ds(at, 1), :] = ref[256:272, :].astype(f32)[0:1, :]

        @pl.when(at == 0)
        def _():
            first[...] = ref[...]


def put_in_order(info, parts):
    whole = pl.BlockSpec(memory_space=pltpu.VMEM)
    return pl.pallas_call(
        order_kernel,
        name="order_keys",
        in_specs=[pl.BlockSpec(memory_space=pltpu.SMEM)] + [whole] * 4,
        out_specs=[whole] * 3,
        out_shape=[
            jax.ShapeDtypeStruct((2, 512, 128), bf16),
            jax.ShapeDtypeStruct((272, 128), bf16),
            jax.ShapeDtypeStruct((8, 128), f32),
        ],
    )(info, *parts)


def forward_kernel(
    info, q0, q1, q2, q3, turns, own, halo, p1, p2, p3, o_ref, l_ref, e_ref, q_s, s_s, t_s
):
    x, z = info[0], info[1]
    for d, ref in enumerate((q0, q1, q2, q3)):
        q_s[slot(x, d), :] = ref[...]

    @pl.when(pl.program_id(0) == 0)
    def _():
        for c in range(4):
            t_s[128 * c : 128 * c + 128, :] = column_of(turns[c : c + 1, :])

    past = (p1, p2, p3)
    halo_turns = halo[256:272, :].astype(f32)[0:1, :]

    def masked(s, b, first_key, count):
        tiles = []
        row = 256 * b + lax.broadcasted_iota(jnp.int32, (256, 128), 0)
        lane = lax.broadcasted_iota(jnp.int32, (256, 128), 1)
        mine = t_s[256 * b : 256 * b + 256, :]
        for j in range(count // 128):
            c = first_key // 128 + j
            theirs = turns[c : c + 1, :] if c < 4 else halo_turns
            seen = (lane + 128 * c <= row) | (mine == theirs)
            tiles.append(jnp.where(seen, s[:, 128 * j : 128 * j + 128], neg_big))
        return jnp.concatenate(tiles, axis=1)

    def block(b, reach):
        rows = pl.ds(256 * b, 256)
        q = q_s[rows, :]
        spans = []
        if b == 1:
            spans.append((own, 0, 256, 0, False))
        spans.append((own, 256 * b, 384 - 128 * b, 256 * b, True) if b == 0 else (own, 256, 256, 256, True))
        if b == 1:
            spans.append((halo, 0, 128, OWN, True))
        for d in range(reach):
            spans.append((past[d], 0, 512, OWN + HALO + 512 * d, False))
        top = None
        for ref, k0, n, c0, partial in spans:
            keys = ref[0:128, :] if ref is halo else ref[0, k0 : k0 + n, :]
            s = dot_nt(q, keys)
            if partial:
                s = masked(s, b, c0, n)
            s_s[rows, c0 : c0 + n] = s
            for j in range(n // 128):
                t = s[:, 128 * j : 128 * j + 128]
                top = t if top is None else jnp.maximum(top, t)
        top = jnp.max(top, axis=1, keepdims=True) * SCALE_LOG2
        total = mixed = None
        for ref, k0, n, c0, _ in spans:
            e = jnp.exp2(s_s[rows, c0 : c0 + n] * SCALE_LOG2 - top)
            for j in range(n // 128):
                t = e[:, 128 * j : 128 * j + 128]
                total = t if total is None else total + t
            e = e.astype(bf16)
            e_ref[0, rows, c0 : c0 + n] = e
            values = ref[128:256, :] if ref is halo else ref[1, k0 : k0 + n, :]
            t = dot_nn(e, values)
            mixed = t if mixed is None else mixed + t
        total = jnp.sum(total, axis=1, keepdims=True)
        o_ref[rows, :] = mixed / total
        l_ref[rows, :] = jnp.broadcast_to(total, (256, 128))

    for reach in range(4):

        @pl.when(z == reach)
        def _():
            block(0, reach)
            block(1, reach)


def per_head(rows):
    return pl.BlockSpec((rows, 128), lambda g, i: (0, g))


def all_of(*shape):
    return pl.BlockSpec(shape, lambda g, i: (0,) * len(shape))


def forward(info, queries, turns, own, halo, past):
    return pl.pallas_call(
        forward_kernel,
        name="attention_forward",
        grid_spec=pltpu.PrefetchScalarGridSpec(
            num_scalar_prefetch=1,
            grid=(GROUP,),
            in_specs=[per_head(128)] * 4
            + [all_of(8, 128), all_of(2, 512, 128), all_of(272, 128)]
            + [all_of(2, 512, 128)] * 3,
            out_specs=[
                per_head(512),
                per_head(512),
                pl.BlockSpec((1, 512, WIDTH), lambda g, i: (g, 0, 0)),
            ],
            scratch_shapes=[
                pltpu.VMEM((512, 128), bf16),
                pltpu.VMEM((512, WIDTH), f32),
                pltpu.VMEM((512, 128), f32),
            ],
        ),
        out_shape=[
            jax.ShapeDtypeStruct((512, GROUP * HD), f32),
            jax.ShapeDtypeStruct((512, GROUP * HD), f32),
            jax.ShapeDtypeStruct((GROUP, 512, WIDTH), bf16),
        ],
    )(info, *queries, turns, own, halo, *past)


def sums_kernel(info, o_ref, g0, g1, g2, g3, gain_ref, out):
    x = info[0]
    for d, ref in enumerate((g0, g1, g2, g3)):
        square = dotted = None
        rows = slot(x, d)
        for g in range(GROUP):
            at = pl.ds(128 * g, 128)
            o = o_ref[rows, at]
            u = ref[:, at].astype(f32) * gain_ref[:, at]
            square = o * o if square is None else square + o * o
            dotted = u * o if dotted is None else dotted + u * o
        c = (x - d) & 3
        out[pl.ds(c, 1), :] = jnp.sum(jnp.transpose(square), axis=0, keepdims=True)
        out[pl.ds(4 + c, 1), :] = jnp.sum(jnp.transpose(dotted), axis=0, keepdims=True)


def token_sums(info, output, cotangents, gain):
    whole = pl.BlockSpec(memory_space=pltpu.VMEM)
    return pl.pallas_call(
        sums_kernel,
        name="token_sums",
        in_specs=[pl.BlockSpec(memory_space=pltpu.SMEM)] + [whole] * 6,
        out_specs=whole,
        out_shape=jax.ShapeDtypeStruct((8, 128), f32),
    )(info, output, *cotangents, gain)


def normed_kernel(info, o_ref, sums, gain_ref, n0, n1, n2, n3):
    x = info[0]
    for d, ref in enumerate((n0, n1, n2, n3)):
        c = (x - d) & 3
        inverse = column_of(lax.rsqrt(sums[pl.ds(c, 1), :] / FEATURES + eps_norm))
        rows = slot(x, d)
        for g in range(GROUP):
            at = pl.ds(128 * g, 128)
            ref[:, at] = (o_ref[rows, at] * inverse * gain_ref[:, at]).astype(bf16)


def normed_parts(info, output, sums, gain):
    whole = pl.BlockSpec(memory_space=pltpu.VMEM)
    return pl.pallas_call(
        normed_kernel,
        name="normed_parts",
        in_specs=[pl.BlockSpec(memory_space=pltpu.SMEM)] + [whole] * 3,
        out_specs=[whole] * 4,
        out_shape=[jax.ShapeDtypeStruct((128, GROUP * HD), bf16)] * 4,
    )(info, output, sums, gain)


def backward_kernel(
    info, q0, q1, q2, q3, g0, g1, g2, g3, gain_ref, sums, o_ref, l_ref, e_ref,
    own, halo, p1, p2, p3,
    dq0, dq1, dq2, dq3, d_own, d_halo, d_p1, d_p2, d_p3,
    q_s, g_s, dq_s, dk_s, dv_s, r_s, c_s,
):
    x, z = info[0], info[1]
    head = pl.program_id(0)
    for d, (a, b) in enumerate(((q0, g0), (q1, g1), (q2, g2), (q3, g3))):
        q_s[slot(x, d), :] = a[...]
        g_s[slot(x, d), :] = b[...]

    @pl.when(head == 0)
    def _():
        dk_s[...] = jnp.zeros_like(dk_s)
        dv_s[...] = jnp.zeros_like(dv_s)
        for c in range(4):
            inverse = lax.rsqrt(sums[c : c + 1, :] / FEATURES + eps_norm)
            center = sums[4 + c : 5 + c, :] / FEATURES
            r_s[128 * c : 128 * c + 128, :] = column_of(inverse)
            c_s[128 * c : 128 * c + 128, :] = column_of(inverse * inverse * center)

    output = o_ref[...]
    scaled = g_s[...].astype(f32) * gain_ref[...]
    grad = (r_s[...] * (scaled - output * c_s[...]) / l_ref[...]).astype(bf16)
    wide = grad.astype(f32)
    row_dot = jnp.sum(wide * output, axis=1, keepdims=True)
    grad_t = jnp.transpose(wide).astype(bf16)
    query_t = jnp.transpose(q_s[...].astype(f32)).astype(bf16)
    past = (p1, p2, p3)

    def body(reach):
        spans = [(own, 0, 384, 0, 0, 256), (own, 0, 512, 0, 256, 256), (halo, 0, 128, OWN, 256, 256)]
        for d in range(reach):
            spans.append((past[d], 0, 512, OWN + HALO + 512 * d, 0, 512))
        grad_q = [None, None]
        for ref, k0, n, c0, r0, count in spans:
            e = e_ref[0, r0 : r0 + count, c0 : c0 + n]
            keys = ref[0:128, :] if ref is halo else ref[0, k0 : k0 + n, :]
            values = ref[128:256, :] if ref is halo else ref[1, k0 : k0 + n, :]
            grad_p = dot_nt(grad[r0 : r0 + count, :], values)
            grad_s = (e.astype(f32) * (grad_p - row_dot[r0 : r0 + count, :])).astype(bf16)
            t = dot_nn(grad_s, keys)
            for b in range(count // 256):
                i = r0 // 256 + b
                part = t[256 * b : 256 * b + 256]
                grad_q[i] = part if grad_q[i] is None else grad_q[i] + part
            dv_s[:, c0 : c0 + n] += dot_nn(grad_t[:, r0 : r0 + count], e)
            dk_s[:, c0 : c0 + n] += dot_nn(query_t[:, r0 : r0 + count], grad_s)
        dq_s[...] = (jnp.concatenate(grad_q, axis=0) * SCALE).astype(bf16)

    for reach in range(4):

        @pl.when(z == reach)
        def _():
            body(reach)

    for d, ref in enumerate((dq0, dq1, dq2, dq3)):
        ref[...] = dq_s[slot(x, d), :]

    @pl.when(head == GROUP - 1)
    def _():
        starts = (0, OWN, OWN + HALO, OWN + HALO + PAST, OWN + HALO + 2 * PAST)
        for ref, c0 in zip((d_own, d_halo, d_p1, d_p2, d_p3), starts):
            n = ref.shape[1]
            ref[0] = jnp.transpose(dk_s[:, c0 : c0 + n] * SCALE).astype(ref.dtype)
            ref[1] = jnp.transpose(dv_s[:, c0 : c0 + n]).astype(ref.dtype)


def backward(info, queries, cotangents, gain, sums, output, totals, weights, own, halo, past):
    key_part = jax.ShapeDtypeStruct((2, 512, 128), bf16)
    return pl.pallas_call(
        backward_kernel,
        name="attention_backward",
        grid_spec=pltpu.PrefetchScalarGridSpec(
            num_scalar_prefetch=1,
            grid=(GROUP,),
            in_specs=[per_head(128)] * 8
            + [per_head(1), all_of(8, 128), per_head(512), per_head(512)]
            + [pl.BlockSpec((1, 512, WIDTH), lambda g, i: (g, 0, 0))]
            + [all_of(2, 512, 128), all_of(272, 128)]
            + [all_of(2, 512, 128)] * 3,
            out_specs=[per_head(128)] * 4
            + [all_of(2, 512, 128), all_of(2, 128, 128)]
            + [all_of(2, 512, 128)] * 3,
            scratch_shapes=[pltpu.VMEM((512, 128), bf16)] * 3
            + [pltpu.VMEM((128, WIDTH), f32)] * 2
            + [pltpu.VMEM((512, 128), f32)] * 2,
        ),
        out_shape=[jax.ShapeDtypeStruct((128, GROUP * HD), bf16)] * 4
        + [jax.ShapeDtypeStruct((2, 512, 128), f32), jax.ShapeDtypeStruct((2, 128, 128), bf16)]
        + [key_part] * 3,
    )(info, *queries, *cotangents, gain, sums, output, totals, weights, own, halo, *past)


def along(x, axis, pairs):
    return lax.ppermute(x, axis, pairs)


def to_units(block, x):
    parts = []
    for d in range(4):
        unit = (x + d) & 3
        part = lax.dynamic_slice(
            block, (unit // 2, 0, (unit % 2) * GROUP * HD), (1, 128, GROUP * HD)
        )[0]
        parts.append(part if d == 0 else along(part, "ctx_1", [(i, (i + d) % 4) for i in range(4)]))
    return parts


def from_units(parts, x):
    got = [parts[0]]
    for d in range(1, 4):
        got.append(along(parts[d], "ctx_1", [(i, (i - d) % 4) for i in range(4)]))
    units = jnp.stack(got)
    units = jnp.stack([lax.dynamic_index_in_dim(units, (u - x) & 3, 0, False) for u in range(4)])
    units = units.reshape(2, 2, 128, GROUP * HD)
    return jnp.concatenate([units[:, 0], units[:, 1]], axis=-1)


def section_route(d, sign):
    route = []
    for s in range(4):
        for i in range(4):
            if sign > 0:
                unit = (i + d) % 4
                route.append((s * 4 + i, (s + unit // 2) % 4 * 4 + unit))
            else:
                route.append((s * 4 + i, (s - i // 2) % 4 * 4 + (i - d) % 4))
    return route


def on_device(query_heads, keys_values, grad_output, norm_gain, turn_ids):
    z = lax.axis_index("ctx_0")
    x = lax.axis_index("ctx_1")
    info = jnp.stack([x, z]).astype(jnp.int32)

    turn_rows = jnp.broadcast_to(turn_ids.astype(bf16)[None], (16, 128))
    kv = keys_values[0]
    heads = [
        jnp.concatenate([kv[:, 0, a : a + HD], kv[:, 1, a : a + HD], turn_rows], axis=0)
        for a in (0, HD)
    ]
    odd = (x & 1) == 1
    same = jnp.where(odd, heads[1], heads[0])
    other = jnp.where(odd, heads[0], heads[1])
    received = [
        along(same if d % 2 == 0 else other, ("section", "ctx_1"), section_route(d, 1))
        for d in range(4)
    ]
    queries = to_units(query_heads[0], x)
    own, first, turns = put_in_order(info, received)
    halo = along(first, "ctx_0", [(1, 0), (2, 1), (3, 2)])
    past1 = along(own, "ctx_0", [(0, 1), (1, 2), (2, 3)])
    past2 = along(own, "ctx_0", [(0, 2), (1, 3)])
    past3 = along(past2, "ctx_0", [(2, 3)])
    past = (past1, past2, past3)
    cotangents = to_units(grad_output[0], x)
    gain = lax.dynamic_slice(norm_gain[0], (x // 2, (x % 2) * GROUP * HD), (1, GROUP * HD))

    output, totals, weights = forward(info, queries, turns, own, halo, past)
    sums = token_sums(info, output, cotangents, gain)
    sums = sums + along(sums, "tp", [(i, i ^ 1) for i in range(4)])
    sums = sums + along(sums, "ctx_1", [(i, i ^ 1) for i in range(4)])
    sums = sums + along(sums, "tp", [(i, i ^ 2) for i in range(4)])
    normed = from_units(normed_parts(info, output, sums, gain), x)

    results = backward(
        info, queries, cotangents, gain, sums, output, totals, weights, own, halo, past
    )
    grad_q = from_units(results[:4], x)
    d_own, d_halo, d_p1, d_p2, d_p3 = results[4:]
    back1 = along(d_p1, "ctx_0", [(1, 0), (2, 1), (3, 2)])
    back2 = along(d_p2, "ctx_0", [(2, 0), (3, 1)])
    back3 = along(d_p3, "ctx_0", [(3, 0)])
    front = along(d_halo, "ctx_0", [(0, 1), (1, 2), (2, 3)])
    total = d_own + back1.astype(f32) + back2.astype(f32) + back3.astype(f32)
    total = total + jnp.pad(front.astype(f32), ((0, 0), (0, 384), (0, 0)))
    total = total.astype(bf16).reshape(2, 4, 128, HD)
    returned = []
    for d in range(4):
        part = lax.dynamic_index_in_dim(total, (x - d) & 3, 1, False)
        returned.append(along(part, ("section", "ctx_1"), section_route(d, -1)))
    alike = returned[0].astype(f32) + returned[2].astype(f32)
    differ = returned[1].astype(f32) + returned[3].astype(f32)
    low = jnp.where(odd, differ, alike)
    high = jnp.where(odd, alike, differ)
    kv_grad = jnp.concatenate([low, high], axis=-1).transpose(1, 0, 2)
    return normed[None], grad_q[None], kv_grad[None]


def solution(mesh):
    split = Mesh(
        mesh.devices.reshape(mesh.shape["section"], 4, 4, mesh.shape["tp"]),
        ("section", "ctx_0", "ctx_1", "tp"),
    )
    return jax.shard_map(
        on_device,
        mesh=split,
        in_specs=(
            P("section", None, CTX, "tp"),
            P("section", CTX, None, "tp"),
            P("section", None, CTX, "tp"),
            P("section", None, "tp"),
            P(CTX),
        ),
        out_specs=(
            P("section", None, CTX, "tp"),
            P("section", None, CTX, "tp"),
            P("section", CTX, None, "tp"),
        ),
        check_vma=False,
    )
```

```python
import math

import jax
import jax.numpy as jnp
from jax import lax
from jax.experimental import pallas as pl
from jax.experimental.pallas import tpu as pltpu
from jax.sharding import Mesh
from jax.sharding import PartitionSpec as P


HD = 128
KVH = 8
GROUP = 6
FEATURES = KVH * GROUP * HD
CTX = ("ctx_0", "ctx_1")
OWN, HALO, PAST = 512, 128, 512
NEAR, FAR = OWN + HALO + PAST, 2 * PAST
SCALE = HD**-0.5
SCALE_LOG2 = SCALE * math.log2(math.e)


neg_big = -1e30
eps_norm = 1e-06
bf16 = jnp.bfloat16
f32 = jnp.float32


def dot_nt(a, b):
    return lax.dot_general(a, b, (((1,), (1,)), ((), ())), preferred_element_type=f32)


def dot_nn(a, b):
    return lax.dot_general(a, b, (((1,), (0,)), ((), ())), preferred_element_type=f32)


def slot(x, d):
    return pl.ds(pl.multiple_of(((x - d) & 3) * 128, 128), 128)


def column_of(row):
    return jnp.transpose(jnp.broadcast_to(row, (128, 128)))


def order_kernel(info, a0, a1, a2, a3, own, first, turns):
    x = info[0]
    for d, ref in enumerate((a0, a1, a2, a3)):
        rows = slot(x, d)
        own[0, rows, :] = ref[0:128, :]
        own[1, rows, :] = ref[128:256, :]
        at = (x - d) & 3
        turns[pl.ds(at, 1), :] = ref[256:272, :].astype(f32)[0:1, :]

        @pl.when(at == 0)
        def _():
            first[...] = ref[...]


def put_in_order(info, parts):
    whole = pl.BlockSpec(memory_space=pltpu.VMEM)
    return pl.pallas_call(
        order_kernel,
        name="order_keys",
        in_specs=[pl.BlockSpec(memory_space=pltpu.SMEM)] + [whole] * 4,
        out_specs=[whole] * 3,
        out_shape=[
            jax.ShapeDtypeStruct((2, 512, 128), bf16),
            jax.ShapeDtypeStruct((272, 128), bf16),
            jax.ShapeDtypeStruct((8, 128), f32),
        ],
    )(info, *parts)


KEPT = pl.BlockSpec(memory_space=pltpu.VMEM)
LIMIT = pltpu.CompilerParams(vmem_limit_bytes=28 << 20)


def per_head(rows, at=0):
    return pl.BlockSpec((rows, 128), lambda g, i: (at, g))


def all_of(*shape):
    return pl.BlockSpec(shape, lambda g, i: (0,) * len(shape))


def keys_of(ref, k0, n):
    return ref[k0 : k0 + n, :] if len(ref.shape) == 2 else ref[0, k0 : k0 + n, :]


def values_of(ref, k0, n):
    return ref[128 + k0 : 128 + k0 + n, :] if len(ref.shape) == 2 else ref[1, k0 : k0 + n, :]


def forward_kernel(
    info, q0, q1, q2, q3, g0, g1, g2, g3, gain_ref, turns, own, halo, p1, p2, p3,
    o_ref, l_ref, near_ref, far_ref, sums_ref, q_s, g_s, s_s, t_s, sq_s, dot_s,
):
    x, z = info[0], info[1]
    head = pl.program_id(0)
    for d, (a, b) in enumerate(((q0, g0), (q1, g1), (q2, g2), (q3, g3))):
        q_s[slot(x, d), :] = a[...]
        g_s[slot(x, d), :] = b[...]

    @pl.when(head == 0)
    def _():
        sq_s[...] = jnp.zeros_like(sq_s)
        dot_s[...] = jnp.zeros_like(dot_s)
        for c in range(4):
            t_s[128 * c : 128 * c + 128, :] = column_of(turns[c : c + 1, :])

    halo_turns = halo[256:272, :].astype(f32)[0:1, :]

    def masked(s, b, first_key, count):
        tiles = []
        row = 256 * b + lax.broadcasted_iota(jnp.int32, (256, 128), 0)
        lane = lax.broadcasted_iota(jnp.int32, (256, 128), 1)
        mine = t_s[256 * b : 256 * b + 256, :]
        for j in range(count // 128):
            c = first_key // 128 + j
            theirs = turns[c : c + 1, :] if c < 4 else halo_turns
            seen = (lane + 128 * c <= row) | (mine == theirs)
            tiles.append(jnp.where(seen, s[:, 128 * j : 128 * j + 128], neg_big))
        return jnp.concatenate(tiles, axis=1)

    def block(b, reach):
        rows = pl.ds(256 * b, 256)
        q = q_s[rows, :]
        if b == 0:
            spans = [(own, 0, 384, near_ref, 0, True)]
        else:
            spans = [
                (own, 0, 256, near_ref, 0, False),
                (own, 256, 256, near_ref, 256, True),
                (halo, 0, 128, near_ref, OWN, True),
            ]
        if reach > 0:
            spans.append((p1, 0, 512, near_ref, OWN + HALO, False))
        if reach > 1:
            spans.append((p2, 0, 512, far_ref, 0, False))
        if reach > 2:
            spans.append((p3, 0, 512, far_ref, PAST, False))
        top = None
        for ref, k0, n, to, c0, partial in spans:
            s = dot_nt(q, keys_of(ref, k0, n))
            if partial:
                s = masked(s, b, c0, n)
            at = c0 + (NEAR if to is far_ref else 0)
            s_s[rows, at : at + n] = s
            for j in range(n // 128):
                t = s[:, 128 * j : 128 * j + 128]
                top = t if top is None else jnp.maximum(top, t)
        top = jnp.max(top, axis=1, keepdims=True) * SCALE_LOG2
        total = mixed = None
        for ref, k0, n, to, c0, _ in spans:
            at = c0 + (NEAR if to is far_ref else 0)
            e = jnp.exp2(s_s[rows, at : at + n] * SCALE_LOG2 - top)
            for j in range(n // 128):
                t = e[:, 128 * j : 128 * j + 128]
                total = t if total is None else total + t
            e = e.astype(bf16)
            to[head, rows, c0 : c0 + n] = e
            t = dot_nn(e, values_of(ref, k0, n))
            mixed = t if mixed is None else mixed + t
        total = jnp.sum(total, axis=1, keepdims=True)
        o = mixed / total
        o_ref[head, rows, :] = o
        l_ref[head, rows, :] = jnp.broadcast_to(total, (256, 128))
        sq_s[rows, :] += o * o
        dot_s[rows, :] += g_s[rows, :].astype(f32) * gain_ref[...] * o

    for reach in range(4):

        @pl.when(z == reach)
        def _():
            block(0, reach)
            block(1, reach)

    @pl.when(head == GROUP - 1)
    def _():
        for c in range(4):
            rows = pl.ds(128 * c, 128)
            sums_ref[c : c + 1, :] = jnp.sum(jnp.transpose(sq_s[rows, :]), axis=0, keepdims=True)
            sums_ref[4 + c : 5 + c, :] = jnp.sum(
                jnp.transpose(dot_s[rows, :]), axis=0, keepdims=True
            )


def forward(info, parts, gain, turns, own, halo, past):
    return pl.pallas_call(
        forward_kernel,
        name="attention_forward",
        grid_spec=pltpu.PrefetchScalarGridSpec(
            num_scalar_prefetch=1,
            grid=(GROUP,),
            in_specs=[per_head(128)] * 4
            + [per_head(128, 1)] * 4
            + [per_head(1), all_of(8, 128), all_of(2, 512, 128), all_of(272, 128)]
            + [all_of(2, 512, 128)] * 3,
            out_specs=[KEPT] * 4 + [all_of(8, 128)],
            scratch_shapes=[
                pltpu.VMEM((512, 128), bf16),
                pltpu.VMEM((512, 128), bf16),
                pltpu.VMEM((512, NEAR + FAR), f32),
                pltpu.VMEM((512, 128), f32),
                pltpu.VMEM((512, 128), f32),
                pltpu.VMEM((512, 128), f32),
            ],
        ),
        out_shape=[
            pltpu.VMEM((GROUP, 512, HD), f32),
            pltpu.VMEM((GROUP, 512, HD), f32),
            pltpu.VMEM((GROUP, 512, NEAR), bf16),
            pltpu.VMEM((GROUP, 512, FAR), bf16),
            jax.ShapeDtypeStruct((8, 128), f32),
        ],
        compiler_params=LIMIT,
    )(info, *parts, *parts, gain, turns, own, halo, *past)


def cotangent_rows(q_s, g_s, gain_ref, r_s, c_s, o_ref, l_ref):
    output = o_ref[pl.program_id(0)]
    scaled = g_s[...].astype(f32) * gain_ref[...]
    grad = (r_s[...] * (scaled - output * c_s[...]) / l_ref[pl.program_id(0)]).astype(bf16)
    wide = grad.astype(f32)
    row_dot = jnp.sum(wide * output, axis=1, keepdims=True)
    grad_t = jnp.transpose(wide).astype(bf16)
    query_t = jnp.transpose(q_s[...].astype(f32)).astype(bf16)
    return grad, row_dot, grad_t, query_t


def fill_columns(sums, r_s, c_s):
    for c in range(4):
        inverse = lax.rsqrt(sums[c : c + 1, :] / FEATURES + eps_norm)
        center = sums[4 + c : 5 + c, :] / FEATURES
        r_s[128 * c : 128 * c + 128, :] = column_of(inverse)
        c_s[128 * c : 128 * c + 128, :] = column_of(inverse * inverse * center)


def spans_back(spans, e_ref, rows_of, grad_q, dk_s, dv_s):
    grad, row_dot, grad_t, query_t = rows_of
    for ref, k0, n, c0, r0, count in spans:
        e = e_ref[pl.program_id(0), r0 : r0 + count, c0 : c0 + n]
        grad_p = dot_nt(grad[r0 : r0 + count, :], values_of(ref, k0, n))
        grad_s = (e.astype(f32) * (grad_p - row_dot[r0 : r0 + count, :])).astype(bf16)
        t = dot_nn(grad_s, keys_of(ref, k0, n))
        for b in range(count // 256):
            i = r0 // 256 + b
            part = t[256 * b : 256 * b + 256]
            grad_q[i] = part if grad_q[i] is None else grad_q[i] + part
        dv_s[:, c0 : c0 + n] += dot_nn(grad_t[:, r0 : r0 + count], e)
        dk_s[:, c0 : c0 + n] += dot_nn(query_t[:, r0 : r0 + count], grad_s)


def write_keys(refs, starts, dk_s, dv_s):
    for ref, c0 in zip(refs, starts):
        n = ref.shape[1]
        ref[0] = jnp.transpose(dk_s[:, c0 : c0 + n] * SCALE).astype(ref.dtype)
        ref[1] = jnp.transpose(dv_s[:, c0 : c0 + n]).astype(ref.dtype)


def far_kernel(
    info, q0, q1, q2, q3, g0, g1, g2, g3, gain_ref, sums, o_ref, l_ref, e_ref, p2, p3,
    n0, n1, n2, n3, dq_ref, d_p2, d_p3, q_s, g_s, dk_s, dv_s, r_s, c_s,
):
    x, z = info[0], info[1]
    head = pl.program_id(0)

    @pl.when(head == 0)
    def _():
        dk_s[...] = jnp.zeros_like(dk_s)
        dv_s[...] = jnp.zeros_like(dv_s)
        fill_columns(sums, r_s, c_s)

    for d, ref in enumerate((n0, n1, n2, n3)):
        rows = slot(x, d)
        ref[...] = (o_ref[head, rows, :] * r_s[rows, :] * gain_ref[...]).astype(bf16)

    @pl.when(z < 2)
    def _():
        dq_ref[head] = jnp.zeros((512, HD), f32)

    for reach in (2, 3):

        @pl.when(z == reach)
        def _():
            for d, (a, b) in enumerate(((q0, g0), (q1, g1), (q2, g2), (q3, g3))):
                q_s[slot(x, d), :] = a[...]
                g_s[slot(x, d), :] = b[...]
            rows_of = cotangent_rows(q_s, g_s, gain_ref, r_s, c_s, o_ref, l_ref)
            spans = [(p2, 0, 512, 0, 0, 512), (p3, 0, 512, PAST, 0, 512)][: reach - 1]
            grad_q = [None, None]
            spans_back(spans, e_ref, rows_of, grad_q, dk_s, dv_s)
            dq_ref[head] = jnp.concatenate(grad_q, axis=0)

    @pl.when((head == GROUP - 1) & (z > 1))
    def _():
        write_keys((d_p2, d_p3), (0, PAST), dk_s, dv_s)


def backward_far(info, parts, gain, sums, output, totals, weights, p2, p3):
    return pl.pallas_call(
        far_kernel,
        name="backward_far",
        grid_spec=pltpu.PrefetchScalarGridSpec(
            num_scalar_prefetch=1,
            grid=(GROUP,),
            in_specs=[per_head(128)] * 4
            + [per_head(128, 1)] * 4
            + [per_head(1), all_of(8, 128), KEPT, KEPT, KEPT]
            + [all_of(2, 512, 128)] * 2,
            out_specs=[per_head(128)] * 4 + [KEPT] + [all_of(2, 512, 128)] * 2,
            scratch_shapes=[pltpu.VMEM((512, 128), bf16)] * 2
            + [pltpu.VMEM((128, FAR), f32)] * 2
            + [pltpu.VMEM((512, 128), f32)] * 2,
        ),
        out_shape=[jax.ShapeDtypeStruct((128, GROUP * HD), bf16)] * 4
        + [pltpu.VMEM((GROUP, 512, HD), f32)]
        + [jax.ShapeDtypeStruct((2, 512, 128), bf16)] * 2,
        compiler_params=LIMIT,
    )(info, *parts, *parts, gain, sums, output, totals, weights, p2, p3)


def near_kernel(
    info, q0, q1, q2, q3, g0, g1, g2, g3, gain_ref, sums, o_ref, l_ref, e_ref, dq_ref,
    own, halo, p1,
    dq0, dq1, dq2, dq3, d_own, d_halo, d_p1, q_s, g_s, dq_s, dk_s, dv_s, r_s, c_s,
):
    x, z = info[0], info[1]
    head = pl.program_id(0)
    for d, (a, b) in enumerate(((q0, g0), (q1, g1), (q2, g2), (q3, g3))):
        q_s[slot(x, d), :] = a[...]
        g_s[slot(x, d), :] = b[...]

    @pl.when(head == 0)
    def _():
        dk_s[...] = jnp.zeros_like(dk_s)
        dv_s[...] = jnp.zeros_like(dv_s)
        fill_columns(sums, r_s, c_s)

    rows_of = cotangent_rows(q_s, g_s, gain_ref, r_s, c_s, o_ref, l_ref)

    def body(reach):
        spans = [
            (own, 0, 384, 0, 0, 256),
            (own, 0, 512, 0, 256, 256),
            (halo, 0, 128, OWN, 256, 256),
        ]
        if reach:
            spans.append((p1, 0, 512, OWN + HALO, 0, 512))
        grad_q = [dq_ref[head, 0:256, :], dq_ref[head, 256:512, :]]
        spans_back(spans, e_ref, rows_of, grad_q, dk_s, dv_s)
        dq_s[...] = (jnp.concatenate(grad_q, axis=0) * SCALE).astype(bf16)

    @pl.when(z == 0)
    def _():
        body(0)

    @pl.when(z > 0)
    def _():
        body(1)

    for d, ref in enumerate((dq0, dq1, dq2, dq3)):
        ref[...] = dq_s[slot(x, d), :]

    @pl.when(head == GROUP - 1)
    def _():
        write_keys((d_own, d_halo, d_p1), (0, OWN, OWN + HALO), dk_s, dv_s)


def backward_near(info, parts, gain, sums, output, totals, weights, dq, own, halo, p1):
    return pl.pallas_call(
        near_kernel,
        name="backward_near",
        grid_spec=pltpu.PrefetchScalarGridSpec(
            num_scalar_prefetch=1,
            grid=(GROUP,),
            in_specs=[per_head(128)] * 4
            + [per_head(128, 1)] * 4
            + [per_head(1), all_of(8, 128), KEPT, KEPT, KEPT]
            + [KEPT, all_of(2, 512, 128), all_of(272, 128), all_of(2, 512, 128)],
            out_specs=[per_head(128)] * 4
            + [all_of(2, 512, 128), all_of(2, 128, 128), all_of(2, 512, 128)],
            scratch_shapes=[pltpu.VMEM((512, 128), bf16)] * 3
            + [pltpu.VMEM((128, NEAR), f32)] * 2
            + [pltpu.VMEM((512, 128), f32)] * 2,
        ),
        out_shape=[jax.ShapeDtypeStruct((128, GROUP * HD), bf16)] * 4
        + [
            jax.ShapeDtypeStruct((2, 512, 128), f32),
            jax.ShapeDtypeStruct((2, 128, 128), bf16),
            jax.ShapeDtypeStruct((2, 512, 128), bf16),
        ],
        compiler_params=LIMIT,
    )(info, *parts, *parts, gain, sums, output, totals, weights, dq, own, halo, p1)


def along(x, axis, pairs):
    return lax.ppermute(x, axis, pairs)


def unit_of(block, unit):
    return lax.dynamic_slice(
        block, (unit // 2, 0, (unit % 2) * GROUP * HD), (1, 128, GROUP * HD)
    )[0]


def to_units(first, second, x):
    parts = []
    for d in range(4):
        unit = (x + d) & 3
        part = jnp.concatenate([unit_of(first, unit), unit_of(second, unit)], axis=0)
        parts.append(
            part if d == 0 else along(part, "ctx_1", [(i, (i + d) % 4) for i in range(4)])
        )
    return parts


def from_units(parts, x):
    got = [parts[0]]
    for d in range(1, 4):
        got.append(along(parts[d], "ctx_1", [(i, (i - d) % 4) for i in range(4)]))
    units = jnp.stack(got)
    units = jnp.stack([lax.dynamic_index_in_dim(units, (u - x) & 3, 0, False) for u in range(4)])
    units = units.reshape(2, 2, 128, GROUP * HD)
    return jnp.concatenate([units[:, 0], units[:, 1]], axis=-1)


def section_route(d, sign):
    route = []
    for s in range(4):
        for i in range(4):
            if sign > 0:
                unit = (i + d) % 4
                route.append((s * 4 + i, (s + unit // 2) % 4 * 4 + unit))
            else:
                route.append((s * 4 + i, (s - i // 2) % 4 * 4 + (i - d) % 4))
    return route


def whole_step(query_heads, keys_values, grad_output, norm_gain, turn_ids):
    z = lax.axis_index("ctx_0")
    x = lax.axis_index("ctx_1")
    info = jnp.stack([x, z]).astype(jnp.int32)

    turn_rows = jnp.broadcast_to(turn_ids.astype(bf16)[None], (16, 128))
    kv = keys_values[0]
    heads = [
        jnp.concatenate([kv[:, 0, a : a + HD], kv[:, 1, a : a + HD], turn_rows], axis=0)
        for a in (0, HD)
    ]
    odd = (x & 1) == 1
    same = jnp.where(odd, heads[1], heads[0])
    other = jnp.where(odd, heads[0], heads[1])
    received = [
        along(same if d % 2 == 0 else other, ("section", "ctx_1"), section_route(d, 1))
        for d in range(4)
    ]
    parts = to_units(query_heads[0], grad_output[0], x)
    own, first, turns = put_in_order(info, received)
    halo = along(first, "ctx_0", [(1, 0), (2, 1), (3, 2)])
    past2 = along(own, "ctx_0", [(0, 2), (1, 3)])
    past1 = along(own, "ctx_0", [(0, 1), (1, 2), (2, 3)])
    past3 = along(past2, "ctx_0", [(2, 3)])
    gain = lax.dynamic_slice(norm_gain[0], (x // 2, (x % 2) * GROUP * HD), (1, GROUP * HD))

    output, totals, near, far, sums = forward(
        info, parts, gain, turns, own, halo, (past1, past2, past3)
    )
    sums = sums + along(sums, "tp", [(i, i ^ 1) for i in range(4)])
    sums = sums + along(sums, "ctx_1", [(i, i ^ 1) for i in range(4)])
    sums = sums + along(sums, "tp", [(i, i ^ 2) for i in range(4)])

    results = backward_far(info, parts, gain, sums, output, totals, far, past2, past3)
    d_p2, d_p3 = results[5:]
    back3 = along(d_p3, "ctx_0", [(3, 0)])
    back2 = along(d_p2, "ctx_0", [(2, 0), (3, 1)])
    normed = from_units(results[:4], x)
    results = backward_near(
        info, parts, gain, sums, output, totals, near, results[4], own, halo, past1
    )
    d_own, d_halo, d_p1 = results[4:]
    back1 = along(d_p1, "ctx_0", [(1, 0), (2, 1), (3, 2)])
    front = along(d_halo, "ctx_0", [(0, 1), (1, 2), (2, 3)])
    grad_q = from_units(results[:4], x)
    total = d_own + back1.astype(f32) + back2.astype(f32) + back3.astype(f32)
    total = total + jnp.pad(front.astype(f32), ((0, 0), (0, 384), (0, 0)))
    total = total.astype(bf16).reshape(2, 4, 128, HD)
    returned = []
    for d in range(4):
        part = lax.dynamic_index_in_dim(total, (x - d) & 3, 1, False)
        returned.append(along(part, ("section", "ctx_1"), section_route(d, -1)))
    alike = returned[0].astype(f32) + returned[2].astype(f32)
    differ = returned[1].astype(f32) + returned[3].astype(f32)
    low = jnp.where(odd, differ, alike)
    high = jnp.where(odd, alike, differ)
    kv_grad = jnp.concatenate([low, high], axis=-1).transpose(1, 0, 2)
    return normed[None], grad_q[None], kv_grad[None]


def solution(mesh):
    split = Mesh(
        mesh.devices.reshape(mesh.shape["section"], 4, 4, mesh.shape["tp"]),
        ("section", "ctx_0", "ctx_1", "tp"),
    )
    return jax.shard_map(
        whole_step,
        mesh=split,
        in_specs=(
            P("section", None, CTX, "tp"),
            P("section", CTX, None, "tp"),
            P("section", None, CTX, "tp"),
            P("section", None, "tp"),
            P(CTX),
        ),
        out_specs=(
            P("section", None, CTX, "tp"),
            P("section", None, CTX, "tp"),
            P("section", CTX, None, "tp"),
        ),
        check_vma=False,
    )
```

```python
import math

import jax
import jax.numpy as jnp
from jax import lax
from jax.experimental import pallas as pl
from jax.experimental.pallas import tpu as pltpu
from jax.sharding import Mesh
from jax.sharding import PartitionSpec as P


HD = 128
KVH = 8
GROUP = 6
FEATURES = KVH * GROUP * HD
CTX = ("ctx_0", "ctx_1")
OWN, HALO, PAST = 512, 128, 512
NEAR, FAR = OWN + HALO + PAST, 2 * PAST
SCALE = HD**-0.5
SCALE_LOG2 = SCALE * math.log2(math.e)


neg_big = -1e30
eps_norm = 1e-06
bf16 = jnp.bfloat16
f32 = jnp.float32


KEPT = pl.BlockSpec(memory_space=pltpu.VMEM)
SCALARS = pl.BlockSpec(memory_space=pltpu.SMEM)
LIMIT = pltpu.CompilerParams(vmem_limit_bytes=28 << 20)


def dot_nt(a, b):
    return lax.dot_general(a, b, (((1,), (1,)), ((), ())), preferred_element_type=f32)


def dot_nn(a, b):
    return lax.dot_general(a, b, (((1,), (0,)), ((), ())), preferred_element_type=f32)


def slot(x, d):
    return pl.ds(pl.multiple_of(((x - d) & 3) * 128, 128), 128)


def column_of(row):
    return jnp.transpose(jnp.broadcast_to(row, (128, 128)))


def order_kernel(info, a0, a1, a2, a3, own, first, turns):
    x = info[0]
    for d, ref in enumerate((a0, a1, a2, a3)):
        rows = slot(x, d)
        own[0, rows, :] = ref[0:128, :]
        own[1, rows, :] = ref[128:256, :]
        at = (x - d) & 3
        turns[pl.ds(at, 1), :] = ref[256:272, :].astype(f32)[0:1, :]

        @pl.when(at == 0)
        def _():
            first[...] = ref[...]


def put_in_order(info, parts):
    whole = pl.BlockSpec(memory_space=pltpu.VMEM)
    return pl.pallas_call(
        order_kernel,
        name="order_keys",
        in_specs=[pl.BlockSpec(memory_space=pltpu.SMEM)] + [whole] * 4,
        out_specs=[whole] * 3,
        out_shape=[
            pltpu.VMEM((2, 512, 128), bf16),
            pltpu.VMEM((272, 128), bf16),
            pltpu.VMEM((8, 128), f32),
        ],
        compiler_params=LIMIT,
    )(info, *parts)


def per_head(rows, at=0):
    return pl.BlockSpec((rows, 128), lambda g, i: (at, g))


def all_of(*shape):
    return pl.BlockSpec(shape, lambda g, i: (0,) * len(shape))


def keys_of(ref, k0, n):
    return ref[k0 : k0 + n, :] if len(ref.shape) == 2 else ref[0, k0 : k0 + n, :]


def values_of(ref, k0, n):
    return ref[128 + k0 : 128 + k0 + n, :] if len(ref.shape) == 2 else ref[1, k0 : k0 + n, :]


def forward_kernel(
    info, q0, q1, q2, q3, g0, g1, g2, g3, gain_ref, turns, own, halo, p1, p2, p3,
    o_ref, l_ref, near_ref, far_ref, sums_ref, q_s, g_s, s_s, t_s, sq_s, dot_s,
):
    x, z = info[0], info[1]
    head = pl.program_id(0)
    for d, (a, b) in enumerate(((q0, g0), (q1, g1), (q2, g2), (q3, g3))):
        q_s[slot(x, d), :] = a[...]
        g_s[slot(x, d), :] = b[...]

    @pl.when(head == 0)
    def _():
        sq_s[...] = jnp.zeros_like(sq_s)
        dot_s[...] = jnp.zeros_like(dot_s)
        for c in range(4):
            t_s[128 * c : 128 * c + 128, :] = column_of(turns[c : c + 1, :])

    halo_turns = halo[256:272, :].astype(f32)[0:1, :]

    def masked(s, b, first_key, count):
        tiles = []
        row = 256 * b + lax.broadcasted_iota(jnp.int32, (256, 128), 0)
        lane = lax.broadcasted_iota(jnp.int32, (256, 128), 1)
        mine = t_s[256 * b : 256 * b + 256, :]
        for j in range(count // 128):
            c = first_key // 128 + j
            theirs = turns[c : c + 1, :] if c < 4 else halo_turns
            seen = (lane + 128 * c <= row) | (mine == theirs)
            tiles.append(jnp.where(seen, s[:, 128 * j : 128 * j + 128], neg_big))
        return jnp.concatenate(tiles, axis=1)

    def block(b, reach):
        rows = pl.ds(256 * b, 256)
        q = q_s[rows, :]
        if b == 0:
            spans = [(own, 0, 384, near_ref, 0, True)]
        else:
            spans = [
                (own, 0, 256, near_ref, 0, False),
                (own, 256, 256, near_ref, 256, True),
                (halo, 0, 128, near_ref, OWN, True),
            ]
        if reach > 0:
            spans.append((p1, 0, 512, near_ref, OWN + HALO, False))
        if reach > 1:
            spans.append((p2, 0, 512, far_ref, 0, False))
        if reach > 2:
            spans.append((p3, 0, 512, far_ref, PAST, False))
        top = None
        for ref, k0, n, to, c0, partial in spans:
            s = dot_nt(q, keys_of(ref, k0, n))
            if partial:
                s = masked(s, b, c0, n)
            at = c0 + (NEAR if to is far_ref else 0)
            s_s[rows, at : at + n] = s
            for j in range(n // 128):
                t = s[:, 128 * j : 128 * j + 128]
                top = t if top is None else jnp.maximum(top, t)
        top = jnp.max(top, axis=1, keepdims=True) * SCALE_LOG2
        total = mixed = None
        for ref, k0, n, to, c0, _ in spans:
            at = c0 + (NEAR if to is far_ref else 0)
            e = jnp.exp2(s_s[rows, at : at + n] * SCALE_LOG2 - top)
            for j in range(n // 128):
                t = e[:, 128 * j : 128 * j + 128]
                total = t if total is None else total + t
            e = e.astype(bf16)
            to[head, rows, c0 : c0 + n] = e
            t = dot_nn(e, values_of(ref, k0, n))
            mixed = t if mixed is None else mixed + t
        total = jnp.sum(total, axis=1, keepdims=True)
        o = mixed / total
        o_ref[head, rows, :] = o
        l_ref[head, rows, :] = jnp.broadcast_to(total, (256, 128))
        sq_s[rows, :] += o * o
        dot_s[rows, :] += g_s[rows, :].astype(f32) * gain_ref[...] * o

    for reach in range(4):

        @pl.when(z == reach)
        def _():
            block(0, reach)
            block(1, reach)

    @pl.when(head == GROUP - 1)
    def _():
        for c in range(4):
            rows = pl.ds(128 * c, 128)
            sums_ref[c : c + 1, :] = jnp.sum(jnp.transpose(sq_s[rows, :]), axis=0, keepdims=True)
            sums_ref[4 + c : 5 + c, :] = jnp.sum(
                jnp.transpose(dot_s[rows, :]), axis=0, keepdims=True
            )


def forward(info, parts, gain, turns, own, halo, past):
    return pl.pallas_call(
        forward_kernel,
        name="attention_forward",
        grid_spec=pltpu.PrefetchScalarGridSpec(
            num_scalar_prefetch=1,
            grid=(GROUP,),
            in_specs=[per_head(128)] * 4
            + [per_head(128, 1)] * 4
            + [per_head(1), all_of(8, 128), all_of(2, 512, 128), all_of(272, 128)]
            + [all_of(2, 512, 128)] * 3,
            out_specs=[KEPT] * 4 + [all_of(8, 128)],
            scratch_shapes=[
                pltpu.VMEM((512, 128), bf16),
                pltpu.VMEM((512, 128), bf16),
                pltpu.VMEM((512, NEAR + FAR), f32),
                pltpu.VMEM((512, 128), f32),
                pltpu.VMEM((512, 128), f32),
                pltpu.VMEM((512, 128), f32),
            ],
        ),
        out_shape=[
            pltpu.VMEM((GROUP, 512, HD), f32),
            pltpu.VMEM((GROUP, 512, HD), f32),
            pltpu.VMEM((GROUP, 512, NEAR), bf16),
            pltpu.VMEM((GROUP, 512, FAR), bf16),
            jax.ShapeDtypeStruct((8, 128), f32),
        ],
        compiler_params=LIMIT,
    )(info, *parts, *parts, gain, turns, own, halo, *past)


def cotangent_rows(q_s, g_s, gain_ref, r_s, c_s, o_ref, l_ref):
    output = o_ref[pl.program_id(0)]
    scaled = g_s[...].astype(f32) * gain_ref[...]
    grad = (r_s[...] * (scaled - output * c_s[...]) / l_ref[pl.program_id(0)]).astype(bf16)
    wide = grad.astype(f32)
    row_dot = jnp.sum(wide * output, axis=1, keepdims=True)
    grad_t = jnp.transpose(wide).astype(bf16)
    query_t = jnp.transpose(q_s[...].astype(f32)).astype(bf16)
    return grad, row_dot, grad_t, query_t


def fill_columns(sums, r_s, c_s):
    for c in range(4):
        inverse = lax.rsqrt(sums[c : c + 1, :] / FEATURES + eps_norm)
        center = sums[4 + c : 5 + c, :] / FEATURES
        r_s[128 * c : 128 * c + 128, :] = column_of(inverse)
        c_s[128 * c : 128 * c + 128, :] = column_of(inverse * inverse * center)


def spans_back(spans, e_ref, rows_of, grad_q, dk_s, dv_s):
    grad, row_dot, grad_t, query_t = rows_of
    for ref, k0, n, c0, r0, count in spans:
        e = e_ref[pl.program_id(0), r0 : r0 + count, c0 : c0 + n]
        grad_p = dot_nt(grad[r0 : r0 + count, :], values_of(ref, k0, n))
        grad_s = (e.astype(f32) * (grad_p - row_dot[r0 : r0 + count, :])).astype(bf16)
        t = dot_nn(grad_s, keys_of(ref, k0, n))
        for b in range(count // 256):
            i = r0 // 256 + b
            part = t[256 * b : 256 * b + 256]
            grad_q[i] = part if grad_q[i] is None else grad_q[i] + part
        dv_s[:, c0 : c0 + n] += dot_nn(grad_t[:, r0 : r0 + count], e)
        dk_s[:, c0 : c0 + n] += dot_nn(query_t[:, r0 : r0 + count], grad_s)


def write_keys(refs, starts, dk_s, dv_s):
    for ref, c0 in zip(refs, starts):
        n = ref.shape[2]
        ref[0] = (dk_s[:, c0 : c0 + n] * SCALE).astype(ref.dtype)
        ref[1] = dv_s[:, c0 : c0 + n].astype(ref.dtype)


def far_kernel(
    info, q0, q1, q2, q3, g0, g1, g2, g3, gain_ref, sums, o_ref, l_ref, e_ref, p2, p3,
    n0, n1, n2, n3, dq_ref, d_p2, d_p3, q_s, g_s, dk_s, dv_s, r_s, c_s,
):
    x, z = info[0], info[1]
    head = pl.program_id(0)

    @pl.when(head == 0)
    def _():
        dk_s[...] = jnp.zeros_like(dk_s)
        dv_s[...] = jnp.zeros_like(dv_s)
        fill_columns(sums, r_s, c_s)

    for d, ref in enumerate((n0, n1, n2, n3)):
        rows = slot(x, d)
        ref[...] = (o_ref[head, rows, :] * r_s[rows, :] * gain_ref[...]).astype(bf16)

    @pl.when(z < 2)
    def _():
        dq_ref[head] = jnp.zeros((512, HD), f32)

    for reach in (2, 3):

        @pl.when(z == reach)
        def _():
            for d, (a, b) in enumerate(((q0, g0), (q1, g1), (q2, g2), (q3, g3))):
                q_s[slot(x, d), :] = a[...]
                g_s[slot(x, d), :] = b[...]
            rows_of = cotangent_rows(q_s, g_s, gain_ref, r_s, c_s, o_ref, l_ref)
            spans = [(p2, 0, 512, 0, 0, 512), (p3, 0, 512, PAST, 0, 512)][: reach - 1]
            grad_q = [None, None]
            spans_back(spans, e_ref, rows_of, grad_q, dk_s, dv_s)
            dq_ref[head] = jnp.concatenate(grad_q, axis=0)

    @pl.when((head == GROUP - 1) & (z > 1))
    def _():
        write_keys((d_p2, d_p3), (0, PAST), dk_s, dv_s)


def backward_far(info, parts, gain, sums, output, totals, weights, p2, p3):
    return pl.pallas_call(
        far_kernel,
        name="backward_far",
        grid_spec=pltpu.PrefetchScalarGridSpec(
            num_scalar_prefetch=1,
            grid=(GROUP,),
            in_specs=[per_head(128)] * 4
            + [per_head(128, 1)] * 4
            + [per_head(1), all_of(8, 128), KEPT, KEPT, KEPT]
            + [all_of(2, 512, 128)] * 2,
            out_specs=[per_head(128)] * 4 + [KEPT] + [KEPT] * 2,
            scratch_shapes=[pltpu.VMEM((512, 128), bf16)] * 2
            + [pltpu.VMEM((128, FAR), f32)] * 2
            + [pltpu.VMEM((512, 128), f32)] * 2,
        ),
        out_shape=[jax.ShapeDtypeStruct((128, GROUP * HD), bf16)] * 4
        + [pltpu.VMEM((GROUP, 512, HD), f32)]
        + [pltpu.VMEM((2, 128, 512), bf16)] * 2,
        compiler_params=LIMIT,
    )(info, *parts, *parts, gain, sums, output, totals, weights, p2, p3)


def near_kernel(
    info, q0, q1, q2, q3, g0, g1, g2, g3, gain_ref, sums, o_ref, l_ref, e_ref, dq_ref,
    own, halo, p1,
    dq0, dq1, dq2, dq3, d_own, d_halo, d_p1, q_s, g_s, dq_s, dk_s, dv_s, r_s, c_s,
):
    x, z = info[0], info[1]
    head = pl.program_id(0)
    for d, (a, b) in enumerate(((q0, g0), (q1, g1), (q2, g2), (q3, g3))):
        q_s[slot(x, d), :] = a[...]
        g_s[slot(x, d), :] = b[...]

    @pl.when(head == 0)
    def _():
        dk_s[...] = jnp.zeros_like(dk_s)
        dv_s[...] = jnp.zeros_like(dv_s)
        fill_columns(sums, r_s, c_s)

    rows_of = cotangent_rows(q_s, g_s, gain_ref, r_s, c_s, o_ref, l_ref)

    def body(reach):
        spans = [
            (own, 0, 384, 0, 0, 256),
            (own, 0, 512, 0, 256, 256),
            (halo, 0, 128, OWN, 256, 256),
        ]
        if reach:
            spans.append((p1, 0, 512, OWN + HALO, 0, 512))
        grad_q = [dq_ref[head, 0:256, :], dq_ref[head, 256:512, :]]
        spans_back(spans, e_ref, rows_of, grad_q, dk_s, dv_s)
        dq_s[...] = (jnp.concatenate(grad_q, axis=0) * SCALE).astype(bf16)

    @pl.when(z == 0)
    def _():
        body(0)

    @pl.when(z > 0)
    def _():
        body(1)

    for d, ref in enumerate((dq0, dq1, dq2, dq3)):
        ref[...] = dq_s[slot(x, d), :]

    @pl.when(head == GROUP - 1)
    def _():
        write_keys((d_own, d_halo, d_p1), (0, OWN, OWN + HALO), dk_s, dv_s)


def backward_near(info, parts, gain, sums, output, totals, weights, dq, own, halo, p1):
    return pl.pallas_call(
        near_kernel,
        name="backward_near",
        grid_spec=pltpu.PrefetchScalarGridSpec(
            num_scalar_prefetch=1,
            grid=(GROUP,),
            in_specs=[per_head(128)] * 4
            + [per_head(128, 1)] * 4
            + [per_head(1), all_of(8, 128), KEPT, KEPT, KEPT]
            + [KEPT, all_of(2, 512, 128), all_of(272, 128), all_of(2, 512, 128)],
            out_specs=[per_head(128)] * 4
            + [KEPT] * 3,
            scratch_shapes=[pltpu.VMEM((512, 128), bf16)] * 3
            + [pltpu.VMEM((128, NEAR), f32)] * 2
            + [pltpu.VMEM((512, 128), f32)] * 2,
        ),
        out_shape=[jax.ShapeDtypeStruct((128, GROUP * HD), bf16)] * 4
        + [
            pltpu.VMEM((2, 128, 512), f32),
            pltpu.VMEM((2, 128, 128), bf16),
            pltpu.VMEM((2, 128, 512), bf16),
        ],
        compiler_params=LIMIT,
    )(info, *parts, *parts, gain, sums, output, totals, weights, dq, own, halo, p1)


def combine_kernel(info, own, back1, back2, back3, front, r0, r1, r2, r3, total):
    x = info[0]
    for c in range(4):
        at = pl.ds(128 * c, 128)
        part = own[:, :, at] + back1[:, :, at].astype(f32)
        part = part + back2[:, :, at].astype(f32) + back3[:, :, at].astype(f32)
        if c == 0:
            part = part + front[...].astype(f32)
        total[c] = part.astype(bf16)
    for d, ref in enumerate((r0, r1, r2, r3)):
        ref[...] = total[(x - d) & 3]


def combine(info, own, back1, back2, back3, front):
    return pl.pallas_call(
        combine_kernel,
        name="combine",
        in_specs=[SCALARS] + [KEPT] * 5,
        out_specs=[KEPT] * 4,
        out_shape=[pltpu.VMEM((2, 128, 128), bf16)] * 4,
        scratch_shapes=[pltpu.VMEM((4, 2, 128, 128), bf16)],
        compiler_params=LIMIT,
    )(info, own, back1, back2, back3, front)


def finish_kernel(info, r0, r1, r2, r3, out):
    x = info[0]
    for a, b, flip in ((r0, r2, 0), (r1, r3, 1)):
        at = pl.ds(pl.multiple_of(((x + flip) & 1) * 128, 128), 128)
        for half in range(2):
            both = a[half].astype(f32) + b[half].astype(f32)
            out[half, :, at] = jnp.transpose(both)


def finish(info, parts):
    return pl.pallas_call(
        finish_kernel,
        name="finish",
        in_specs=[SCALARS] + [KEPT] * 4,
        out_specs=KEPT,
        out_shape=pltpu.VMEM((2, 128, 256), f32),
        compiler_params=LIMIT,
    )(info, *parts)


def gather_kernel(info, r0, r1, r2, r3, out):
    x = info[0]
    for d, ref in enumerate((r0, r1, r2, r3)):
        unit = (x + d) & 3
        at = pl.ds(pl.multiple_of((unit & 1) * GROUP * HD, 128), GROUP * HD)
        out[unit >> 1, :, at] = ref[...]


def gather(info, parts):
    return pl.pallas_call(
        gather_kernel,
        name="gather",
        in_specs=[SCALARS] + [KEPT] * 4,
        out_specs=KEPT,
        out_shape=jax.ShapeDtypeStruct((2, 128, 2 * GROUP * HD), bf16),
        compiler_params=LIMIT,
    )(info, *parts)


def along(x, axis, pairs):
    return lax.ppermute(x, axis, pairs)


def unit_of(block, unit):
    return lax.dynamic_slice(
        block, (unit // 2, 0, (unit % 2) * GROUP * HD), (1, 128, GROUP * HD)
    )[0]


def to_units(first, second, x):
    parts = []
    for d in range(4):
        unit = (x + d) & 3
        part = jnp.concatenate([unit_of(first, unit), unit_of(second, unit)], axis=0)
        parts.append(
            part if d == 0 else along(part, "ctx_1", [(i, (i + d) % 4) for i in range(4)])
        )
    return parts


def from_units(parts, info):
    got = [parts[0]]
    for d in range(1, 4):
        got.append(along(parts[d], "ctx_1", [(i, (i - d) % 4) for i in range(4)]))
    return gather(info, got)


def section_route(d, sign):
    route = []
    for s in range(4):
        for i in range(4):
            if sign > 0:
                unit = (i + d) % 4
                route.append((s * 4 + i, (s + unit // 2) % 4 * 4 + unit))
            else:
                route.append((s * 4 + i, (s - i // 2) % 4 * 4 + (i - d) % 4))
    return route


def whole_step(query_heads, keys_values, grad_output, norm_gain, turn_ids):
    z = lax.axis_index("ctx_0")
    x = lax.axis_index("ctx_1")
    info = jnp.stack([x, z]).astype(jnp.int32)

    turn_rows = jnp.broadcast_to(turn_ids.astype(bf16)[None], (16, 128))
    kv = keys_values[0]
    heads = [
        jnp.concatenate([kv[:, 0, a : a + HD], kv[:, 1, a : a + HD], turn_rows], axis=0)
        for a in (0, HD)
    ]
    odd = (x & 1) == 1
    same = jnp.where(odd, heads[1], heads[0])
    other = jnp.where(odd, heads[0], heads[1])
    received = [
        along(same if d % 2 == 0 else other, ("section", "ctx_1"), section_route(d, 1))
        for d in range(4)
    ]
    parts = to_units(query_heads[0], grad_output[0], x)
    own, first, turns = put_in_order(info, received)
    halo = along(first, "ctx_0", [(1, 0), (2, 1), (3, 2)])
    past2 = along(own, "ctx_0", [(0, 2), (1, 3)])
    past1 = along(own, "ctx_0", [(0, 1), (1, 2), (2, 3)])
    past3 = along(past2, "ctx_0", [(2, 3)])
    gain = lax.dynamic_slice(norm_gain[0], (x // 2, (x % 2) * GROUP * HD), (1, GROUP * HD))

    output, totals, near, far, sums = forward(
        info, parts, gain, turns, own, halo, (past1, past2, past3)
    )
    sums = sums + along(sums, "tp", [(i, i ^ 1) for i in range(4)])
    sums = sums + along(sums, "ctx_1", [(i, i ^ 1) for i in range(4)])
    sums = sums + along(sums, "tp", [(i, i ^ 2) for i in range(4)])

    results = backward_far(info, parts, gain, sums, output, totals, far, past2, past3)
    d_p2, d_p3 = results[5:]
    back3 = along(d_p3, "ctx_0", [(3, 0)])
    back2 = along(d_p2, "ctx_0", [(2, 0), (3, 1)])
    normed = from_units(results[:4], info)
    results = backward_near(
        info, parts, gain, sums, output, totals, near, results[4], own, halo, past1
    )
    d_own, d_halo, d_p1 = results[4:]
    back1 = along(d_p1, "ctx_0", [(1, 0), (2, 1), (3, 2)])
    front = along(d_halo, "ctx_0", [(0, 1), (1, 2), (2, 3)])
    grad_q = from_units(results[:4], info)
    totals = combine(info, d_own, back1, back2, back3, front)
    returned = [
        along(part, ("section", "ctx_1"), section_route(d, -1))
        for d, part in enumerate(totals)
    ]
    kv_grad = finish(info, returned).transpose(1, 0, 2)
    return normed[None], grad_q[None], kv_grad[None]


def solution(mesh):
    split = Mesh(
        mesh.devices.reshape(mesh.shape["section"], 4, 4, mesh.shape["tp"]),
        ("section", "ctx_0", "ctx_1", "tp"),
    )
    return jax.shard_map(
        whole_step,
        mesh=split,
        in_specs=(
            P("section", None, CTX, "tp"),
            P("section", CTX, None, "tp"),
            P("section", None, CTX, "tp"),
            P("section", None, "tp"),
            P(CTX),
        ),
        out_specs=(
            P("section", None, CTX, "tp"),
            P("section", None, CTX, "tp"),
            P("section", CTX, None, "tp"),
        ),
        check_vma=False,
    )
```

```python
import math

import jax
import jax.numpy as jnp
from jax import lax
from jax.experimental import pallas as pl
from jax.experimental.pallas import tpu as pltpu
from jax.sharding import Mesh
from jax.sharding import PartitionSpec as P


HD = 128
KVH = 8
GROUP = 6
FEATURES = KVH * GROUP * HD
CTX = ("ctx_0", "ctx_1")
OWN, HALO, PAST = 512, 128, 512
NEAR, FAR = OWN + HALO + PAST, 2 * PAST
SCALE = HD**-0.5
SCALE_LOG2 = SCALE * math.log2(math.e)


neg_big = -1e30
eps_norm = 1e-06
bf16 = jnp.bfloat16
f32 = jnp.float32


KEPT = pl.BlockSpec(memory_space=pltpu.VMEM)
SCALARS = pl.BlockSpec(memory_space=pltpu.SMEM)
LIMIT = pltpu.CompilerParams(vmem_limit_bytes=28 << 20)
PACKED = pltpu.CompilerParams(vmem_limit_bytes=28 << 20)


def dot_nt(a, b):
    return lax.dot_general(a, b, (((1,), (1,)), ((), ())), preferred_element_type=f32)


def dot_nn(a, b):
    return lax.dot_general(a, b, (((1,), (0,)), ((), ())), preferred_element_type=f32)


def slot(x, d):
    return pl.ds(pl.multiple_of(((x - d) & 3) * 128, 128), 128)


def at_head(head):
    return pl.ds(pl.multiple_of(head * HD, HD), HD)


def column_of(row):
    return jnp.transpose(jnp.broadcast_to(row, (128, 128)))


def order_kernel(info, a0, a1, a2, a3, own, first, turns):
    x = info[0]
    for d, ref in enumerate((a0, a1, a2, a3)):
        rows = slot(x, d)
        own[0, rows, :] = ref[0:128, :]
        own[1, rows, :] = ref[128:256, :]
        at = (x - d) & 3
        turns[pl.ds(at, 1), :] = ref[256:272, :].astype(f32)[0:1, :]

        @pl.when(at == 0)
        def _():
            first[...] = ref[...]


def put_in_order(info, parts):
    return pl.pallas_call(
        order_kernel,
        name="order_keys",
        in_specs=[SCALARS] + [KEPT] * 4,
        out_specs=[KEPT] * 3,
        out_shape=[
            pltpu.VMEM((2, 512, 128), bf16),
            pltpu.VMEM((272, 128), bf16),
            pltpu.VMEM((8, 128), f32),
        ],
        compiler_params=LIMIT,
    )(info, *parts)


def keys_of(ref, k0, n):
    return ref[k0 : k0 + n, :] if len(ref.shape) == 2 else ref[0, k0 : k0 + n, :]


def values_of(ref, k0, n):
    return ref[128 + k0 : 128 + k0 + n, :] if len(ref.shape) == 2 else ref[1, k0 : k0 + n, :]


def near_weights_kernel(
    info, a0, a1, a2, a3, turns, own, halo, p1, o_ref, l_ref, top_ref, near_ref, q_s, s_s, t_s
):
    x, z = info[0], info[1]
    head = pl.program_id(0)
    for d, ref in enumerate((a0, a1, a2, a3)):
        q_s[slot(x, d), :] = ref[0:128, at_head(head)]

    @pl.when(head == 0)
    def _():
        for c in range(4):
            t_s[128 * c : 128 * c + 128, :] = column_of(turns[c : c + 1, :])

    halo_turns = halo[256:272, :].astype(f32)[0:1, :]

    def masked(s, b, first_key, count):
        tiles = []
        row = 256 * b + lax.broadcasted_iota(jnp.int32, (256, 128), 0)
        lane = lax.broadcasted_iota(jnp.int32, (256, 128), 1)
        mine = t_s[256 * b : 256 * b + 256, :]
        for j in range(count // 128):
            c = first_key // 128 + j
            theirs = turns[c : c + 1, :] if c < 4 else halo_turns
            seen = (lane + 128 * c <= row) | (mine == theirs)
            tiles.append(jnp.where(seen, s[:, 128 * j : 128 * j + 128], neg_big))
        return jnp.concatenate(tiles, axis=1)

    def block(b, reach):
        rows = pl.ds(256 * b, 256)
        q = q_s[rows, :]
        if b == 0:
            spans = [(own, 0, 384, 0, True)]
        else:
            spans = [(own, 0, 256, 0, False), (own, 256, 256, 256, True), (halo, 0, 128, OWN, True)]
        if reach:
            spans.append((p1, 0, 512, OWN + HALO, False))
        top = None
        for ref, k0, n, c0, partial in spans:
            s = dot_nt(q, keys_of(ref, k0, n))
            if partial:
                s = masked(s, b, c0, n)
            s_s[rows, c0 : c0 + n] = s
            for j in range(n // 128):
                t = s[:, 128 * j : 128 * j + 128]
                top = t if top is None else jnp.maximum(top, t)
        top = jnp.max(top, axis=1, keepdims=True) * SCALE_LOG2
        total = mixed = None
        for ref, k0, n, c0, _ in spans:
            e = jnp.exp2(s_s[rows, c0 : c0 + n] * SCALE_LOG2 - top)
            part = tile_sum(e)
            total = part if total is None else total + part
            e = e.astype(bf16)
            near_ref[head, rows, c0 : c0 + n] = e
            t = dot_nn(e, values_of(ref, k0, n))
            mixed = t if mixed is None else mixed + t
        o_ref[head, rows, :] = mixed
        l_ref[head, rows, :] = jnp.broadcast_to(jnp.sum(total, axis=1, keepdims=True), (256, 128))
        top_ref[head, rows, :] = jnp.broadcast_to(top, (256, 128))

    for reach in range(2):

        @pl.when((z > 0) if reach else (z == 0))
        def _():
            block(0, reach)
            block(1, reach)


def forward_near(info, parts, turns, own, halo, p1):
    kept = pltpu.VMEM((GROUP, 512, HD), f32)
    return pl.pallas_call(
        near_weights_kernel,
        name="forward_near",
        grid_spec=pltpu.PrefetchScalarGridSpec(
            num_scalar_prefetch=1,
            grid=(GROUP,),
            in_specs=[KEPT] * 8,
            out_specs=[KEPT] * 4,
            scratch_shapes=[
                pltpu.VMEM((512, 128), bf16),
                pltpu.VMEM((512, NEAR), f32),
                pltpu.VMEM((512, 128), f32),
            ],
        ),
        out_shape=[kept] * 3 + [pltpu.VMEM((GROUP, 512, NEAR), bf16)],
        compiler_params=PACKED,
    )(info, *parts, turns, own, halo, p1)


def tile_sum(e):
    tiles = [e[:, 128 * j : 128 * j + 128] for j in range(e.shape[1] // 128)]
    while len(tiles) > 1:
        tiles = [a + c for a, c in zip(tiles[::2], tiles[1::2])] + tiles[len(tiles) & ~1 :]
    return tiles[0]


def far_weights_kernel(
    info, a0, a1, a2, a3, gain_ref, near_o, near_l, near_top, p2, p3,
    o_ref, inv_ref, near_inv_ref, far_ref, sums_ref, q_s, g_s, s_s, sq_s, dot_s,
):
    x, z = info[0], info[1]
    head = pl.program_id(0)
    for d, ref in enumerate((a0, a1, a2, a3)):
        q_s[slot(x, d), :] = ref[0:128, at_head(head)]
        g_s[slot(x, d), :] = ref[128:256, at_head(head)]

    @pl.when(head == 0)
    def _():
        sq_s[...] = jnp.zeros_like(sq_s)
        dot_s[...] = jnp.zeros_like(dot_s)

    def block(b, reach):
        rows = pl.ds(256 * b, 256)
        mixed = near_o[head, rows, :]
        total = near_l[head, rows, :]
        fade = None
        spans = [(p2, 0), (p3, PAST)][: max(reach - 1, 0)]
        if spans:
            q = q_s[rows, :]
            top = None
            for ref, c0 in spans:
                s = dot_nt(q, keys_of(ref, 0, 512))
                s_s[rows, c0 : c0 + 512] = s
                for j in range(4):
                    t = s[:, 128 * j : 128 * j + 128]
                    top = t if top is None else jnp.maximum(top, t)
            top = jnp.max(top, axis=1, keepdims=True) * SCALE_LOG2
            before = near_top[head, rows, :]
            wide_top = jnp.maximum(before, top)
            top = jnp.max(wide_top, axis=1, keepdims=True)
            fade = jnp.exp2(before - wide_top)
            mixed = mixed * fade
            part = None
            for ref, c0 in spans:
                e = jnp.exp2(s_s[rows, c0 : c0 + 512] * SCALE_LOG2 - top)
                t = tile_sum(e)
                part = t if part is None else part + t
                e = e.astype(bf16)
                far_ref[head, rows, c0 : c0 + 512] = e
                mixed = mixed + dot_nn(e, values_of(ref, 0, 512))
            total = total * fade + jnp.sum(part, axis=1, keepdims=True)
        inverse = 1.0 / total
        o = mixed * inverse
        o_ref[head, rows, :] = o
        inv_ref[head, rows, :] = inverse
        near_inv_ref[head, rows, :] = inverse if fade is None else inverse * fade
        sq_s[rows, :] += o * o
        dot_s[rows, :] += g_s[rows, :].astype(f32) * gain_ref[:, at_head(head)] * o

    for reach in (1, 2, 3):

        @pl.when((z < 2) if reach == 1 else (z == reach))
        def _():
            block(0, reach)
            block(1, reach)

    @pl.when(head == GROUP - 1)
    def _():
        for c in range(4):
            rows = pl.ds(128 * c, 128)
            sums_ref[c : c + 1, :] = jnp.sum(jnp.transpose(sq_s[rows, :]), axis=0, keepdims=True)
            sums_ref[4 + c : 5 + c, :] = jnp.sum(
                jnp.transpose(dot_s[rows, :]), axis=0, keepdims=True
            )


def forward_far(info, parts, gain, near_o, near_l, near_top, p2, p3):
    kept = pltpu.VMEM((GROUP, 512, HD), f32)
    return pl.pallas_call(
        far_weights_kernel,
        name="forward_far",
        grid_spec=pltpu.PrefetchScalarGridSpec(
            num_scalar_prefetch=1,
            grid=(GROUP,),
            in_specs=[KEPT] * 10,
            out_specs=[KEPT] * 5,
            scratch_shapes=[pltpu.VMEM((512, 128), bf16)] * 2
            + [pltpu.VMEM((512, FAR), f32)]
            + [pltpu.VMEM((512, 128), f32)] * 2,
        ),
        out_shape=[kept] * 3 + [pltpu.VMEM((GROUP, 512, FAR), bf16), pltpu.VMEM((8, 128), f32)],
        compiler_params=PACKED,
    )(info, *parts, gain, near_o, near_l, near_top, p2, p3)


def cotangent_rows(q_s, g_s, gain_ref, r_s, c_s, o_ref, l_ref):
    output = o_ref[pl.program_id(0)]
    scaled = g_s[...].astype(f32) * gain_ref[:, at_head(pl.program_id(0))]
    grad = (r_s[...] * (scaled - output * c_s[...]) * l_ref[pl.program_id(0)]).astype(bf16)
    wide = grad.astype(f32)
    row_dot = jnp.sum(wide * output, axis=1, keepdims=True)
    grad_t = jnp.transpose(grad)
    query_t = jnp.transpose(q_s[...])
    return grad, row_dot, grad_t, query_t


def fill_columns(sums, r_s, c_s):
    for c in range(4):
        inverse = lax.rsqrt(sums[c : c + 1, :] / FEATURES + eps_norm)
        center = sums[4 + c : 5 + c, :] / FEATURES
        r_s[128 * c : 128 * c + 128, :] = column_of(inverse)
        c_s[128 * c : 128 * c + 128, :] = column_of(inverse * inverse * center)


def spans_back(spans, e_ref, rows_of, grad_q, dk_s, dv_s):
    grad, row_dot, grad_t, query_t = rows_of
    for ref, k0, n, c0, r0, count in spans:
        e = e_ref[pl.program_id(0), r0 : r0 + count, c0 : c0 + n]
        grad_p = dot_nt(grad[r0 : r0 + count, :], values_of(ref, k0, n))
        grad_s = (e.astype(f32) * (grad_p - row_dot[r0 : r0 + count, :])).astype(bf16)
        t = dot_nn(grad_s, keys_of(ref, k0, n))
        for b in range(count // 256):
            i = r0 // 256 + b
            part = t[256 * b : 256 * b + 256]
            grad_q[i] = part if grad_q[i] is None else grad_q[i] + part
        dv_s[:, c0 : c0 + n] += dot_nn(grad_t[:, r0 : r0 + count], e)
        dk_s[:, c0 : c0 + n] += dot_nn(query_t[:, r0 : r0 + count], grad_s)


def write_keys(refs, starts, dk_s, dv_s):
    for ref, c0 in zip(refs, starts):
        n = ref.shape[2]
        ref[0] = (dk_s[:, c0 : c0 + n] * SCALE).astype(ref.dtype)
        ref[1] = dv_s[:, c0 : c0 + n].astype(ref.dtype)


def far_kernel(
    info, a0, a1, a2, a3, gain_ref, sums, o_ref, l_ref, e_ref, p2, p3,
    n0, n1, n2, n3, dq_ref, d_p2, d_p3, q_s, g_s, dk_s, dv_s, r_s, c_s,
):
    x, z = info[0], info[1]
    head = pl.program_id(0)

    @pl.when(head == 0)
    def _():
        dk_s[...] = jnp.zeros_like(dk_s)
        dv_s[...] = jnp.zeros_like(dv_s)
        fill_columns(sums, r_s, c_s)

    for d, ref in enumerate((n0, n1, n2, n3)):
        rows = slot(x, d)
        ref[:, at_head(head)] = (
            o_ref[head, rows, :] * r_s[rows, :] * gain_ref[:, at_head(head)]
        ).astype(bf16)

    @pl.when(z < 2)
    def _():
        dq_ref[head] = jnp.zeros((512, HD), f32)

    for reach in (2, 3):

        @pl.when(z == reach)
        def _():
            for d, ref in enumerate((a0, a1, a2, a3)):
                q_s[slot(x, d), :] = ref[0:128, at_head(head)]
                g_s[slot(x, d), :] = ref[128:256, at_head(head)]
            rows_of = cotangent_rows(q_s, g_s, gain_ref, r_s, c_s, o_ref, l_ref)
            spans = [(p2, 0, 512, 0, 0, 512), (p3, 0, 512, PAST, 0, 512)][: reach - 1]
            grad_q = [None, None]
            spans_back(spans, e_ref, rows_of, grad_q, dk_s, dv_s)
            dq_ref[head] = jnp.concatenate(grad_q, axis=0)

    @pl.when((head == GROUP - 1) & (z > 1))
    def _():
        write_keys((d_p2, d_p3), (0, PAST), dk_s, dv_s)


def backward_far(info, parts, gain, sums, output, totals, weights, p2, p3):
    return pl.pallas_call(
        far_kernel,
        name="backward_far",
        grid_spec=pltpu.PrefetchScalarGridSpec(
            num_scalar_prefetch=1,
            grid=(GROUP,),
            in_specs=[KEPT] * 11,
            out_specs=[KEPT] * 7,
            scratch_shapes=[pltpu.VMEM((512, 128), bf16)] * 2
            + [pltpu.VMEM((128, FAR), f32)] * 2
            + [pltpu.VMEM((512, 128), f32)] * 2,
        ),
        out_shape=[pltpu.VMEM((128, GROUP * HD), bf16)] * 4
        + [pltpu.VMEM((GROUP, 512, HD), f32)]
        + [pltpu.VMEM((2, 128, 512), bf16)] * 2,
        compiler_params=PACKED,
    )(info, *parts, gain, sums, output, totals, weights, p2, p3)


def near_kernel(
    info, a0, a1, a2, a3, gain_ref, sums, o_ref, l_ref, e_ref, dq_ref,
    own, halo, p1,
    dq0, dq1, dq2, dq3, d_own, d_halo, d_p1, q_s, g_s, dq_s, dk_s, dv_s, r_s, c_s,
):
    x, z = info[0], info[1]
    head = pl.program_id(0)
    for d, ref in enumerate((a0, a1, a2, a3)):
        q_s[slot(x, d), :] = ref[0:128, at_head(head)]
        g_s[slot(x, d), :] = ref[128:256, at_head(head)]

    @pl.when(head == 0)
    def _():
        dk_s[...] = jnp.zeros_like(dk_s)
        dv_s[...] = jnp.zeros_like(dv_s)
        fill_columns(sums, r_s, c_s)

    rows_of = cotangent_rows(q_s, g_s, gain_ref, r_s, c_s, o_ref, l_ref)

    def body(reach):
        spans = [
            (own, 0, 384, 0, 0, 256),
            (own, 0, 512, 0, 256, 256),
            (halo, 0, 128, OWN, 256, 256),
        ]
        if reach:
            spans.append((p1, 0, 512, OWN + HALO, 0, 512))
        grad_q = [dq_ref[head, 0:256, :], dq_ref[head, 256:512, :]]
        spans_back(spans, e_ref, rows_of, grad_q, dk_s, dv_s)
        dq_s[...] = (jnp.concatenate(grad_q, axis=0) * SCALE).astype(bf16)

    @pl.when(z == 0)
    def _():
        body(0)

    @pl.when(z > 0)
    def _():
        body(1)

    for d, ref in enumerate((dq0, dq1, dq2, dq3)):
        ref[:, at_head(head)] = dq_s[slot(x, d), :]

    @pl.when(head == GROUP - 1)
    def _():
        write_keys((d_own, d_halo, d_p1), (0, OWN, OWN + HALO), dk_s, dv_s)


def backward_near(info, parts, gain, sums, output, totals, weights, dq, own, halo, p1):
    return pl.pallas_call(
        near_kernel,
        name="backward_near",
        grid_spec=pltpu.PrefetchScalarGridSpec(
            num_scalar_prefetch=1,
            grid=(GROUP,),
            in_specs=[KEPT] * 13,
            out_specs=[KEPT] * 7,
            scratch_shapes=[pltpu.VMEM((512, 128), bf16)] * 3
            + [pltpu.VMEM((128, NEAR), f32)] * 2
            + [pltpu.VMEM((512, 128), f32)] * 2,
        ),
        out_shape=[pltpu.VMEM((128, GROUP * HD), bf16)] * 4
        + [
            pltpu.VMEM((2, 128, 512), f32),
            pltpu.VMEM((2, 128, 128), bf16),
            pltpu.VMEM((2, 128, 512), bf16),
        ],
        compiler_params=LIMIT,
    )(info, *parts, gain, sums, output, totals, weights, dq, own, halo, p1)


def combine_kernel(info, own, back1, back2, back3, front, r0, r1, r2, r3, total):
    x = info[0]
    for c in range(4):
        at = pl.ds(128 * c, 128)
        part = own[:, :, at] + back1[:, :, at].astype(f32)
        part = part + back2[:, :, at].astype(f32) + back3[:, :, at].astype(f32)
        if c == 0:
            part = part + front[...].astype(f32)
        total[c] = part.astype(bf16)
    for d, ref in enumerate((r0, r1, r2, r3)):
        ref[...] = total[(x - d) & 3]


def combine(info, own, back1, back2, back3, front):
    return pl.pallas_call(
        combine_kernel,
        name="combine",
        in_specs=[SCALARS] + [KEPT] * 5,
        out_specs=[KEPT] * 4,
        out_shape=[pltpu.VMEM((2, 128, 128), bf16)] * 4,
        scratch_shapes=[pltpu.VMEM((4, 2, 128, 128), bf16)],
        compiler_params=LIMIT,
    )(info, own, back1, back2, back3, front)


def finish_kernel(info, r0, r1, r2, r3, out):
    x = info[0]
    for a, b, flip in ((r0, r2, 0), (r1, r3, 1)):
        at = pl.ds(pl.multiple_of(((x + flip) & 1) * 128, 128), 128)
        for half in range(2):
            both = a[half].astype(f32) + b[half].astype(f32)
            out[half, :, at] = jnp.transpose(both)


def finish(info, parts):
    return pl.pallas_call(
        finish_kernel,
        name="finish",
        in_specs=[SCALARS] + [KEPT] * 4,
        out_specs=KEPT,
        out_shape=pltpu.VMEM((2, 128, 256), f32),
        compiler_params=LIMIT,
    )(info, *parts)


def gather_kernel(info, r0, r1, r2, r3, out):
    x = info[0]
    for d, ref in enumerate((r0, r1, r2, r3)):
        unit = (x + d) & 3
        at = pl.ds(pl.multiple_of((unit & 1) * GROUP * HD, 128), GROUP * HD)
        out[unit >> 1, :, at] = ref[...]


def gather(info, parts):
    return pl.pallas_call(
        gather_kernel,
        name="gather",
        in_specs=[SCALARS] + [KEPT] * 4,
        out_specs=KEPT,
        out_shape=jax.ShapeDtypeStruct((2, 128, 2 * GROUP * HD), bf16),
        compiler_params=LIMIT,
    )(info, *parts)


def unit_of(block, unit):
    return lax.dynamic_slice(
        block, (unit // 2, 0, (unit % 2) * GROUP * HD), (1, 128, GROUP * HD)
    )[0]


def to_units(first, second, x):
    parts = []
    for d in range(4):
        unit = (x + d) & 3
        part = jnp.concatenate([unit_of(first, unit), unit_of(second, unit)], axis=0)
        parts.append(
            part if d == 0 else lax.ppermute(part, "ctx_1", [(i, (i + d) % 4) for i in range(4)])
        )
    return parts


def from_units(parts, info):
    got = [parts[0]]
    for d in range(1, 4):
        got.append(lax.ppermute(parts[d], "ctx_1", [(i, (i - d) % 4) for i in range(4)]))
    return gather(info, got)


def section_route(d, sign):
    route = []
    for s in range(4):
        for i in range(4):
            if sign > 0:
                unit = (i + d) % 4
                route.append((s * 4 + i, (s + unit // 2) % 4 * 4 + unit))
            else:
                route.append((s * 4 + i, (s - i // 2) % 4 * 4 + (i - d) % 4))
    return route


def whole_step(query_heads, keys_values, grad_output, norm_gain, turn_ids):
    z = lax.axis_index("ctx_0")
    x = lax.axis_index("ctx_1")
    info = jnp.stack([x, z]).astype(jnp.int32)

    turn_rows = jnp.broadcast_to(turn_ids.astype(bf16)[None], (16, 128))
    kv = keys_values[0]
    heads = [
        jnp.concatenate([kv[:, 0, a : a + HD], kv[:, 1, a : a + HD], turn_rows], axis=0)
        for a in (0, HD)
    ]
    odd = (x & 1) == 1
    same = jnp.where(odd, heads[1], heads[0])
    other = jnp.where(odd, heads[0], heads[1])
    received = [
        lax.ppermute(same if d % 2 == 0 else other, ("section", "ctx_1"), section_route(d, 1))
        for d in range(4)
    ]
    parts = to_units(query_heads[0], grad_output[0], x)
    own, first, turns = put_in_order(info, received)
    halo = lax.ppermute(first, "ctx_0", [(1, 0), (2, 1), (3, 2)])
    past2 = lax.ppermute(own, "ctx_0", [(0, 2), (1, 3)])
    past1 = lax.ppermute(own, "ctx_0", [(0, 1), (1, 2), (2, 3)])
    past3 = lax.ppermute(past2, "ctx_0", [(2, 3)])
    gain = lax.dynamic_slice(norm_gain[0], (x // 2, (x % 2) * GROUP * HD), (1, GROUP * HD))

    near_o, near_l, near_top, near = forward_near(info, parts, turns, own, halo, past1)
    output, inverse, near_inverse, far, sums = forward_far(
        info, parts, gain, near_o, near_l, near_top, past2, past3
    )
    sums = sums + lax.ppermute(sums, "tp", [(i, i ^ 1) for i in range(4)])
    sums = sums + lax.ppermute(sums, "ctx_1", [(i, i ^ 1) for i in range(4)])
    sums = sums + lax.ppermute(sums, "tp", [(i, i ^ 2) for i in range(4)])

    results = backward_far(info, parts, gain, sums, output, inverse, far, past2, past3)
    d_p2, d_p3 = results[5:]
    back3 = lax.ppermute(d_p3, "ctx_0", [(3, 0)])
    back2 = lax.ppermute(d_p2, "ctx_0", [(2, 0), (3, 1)])
    normed = from_units(results[:4], info)
    results = backward_near(
        info, parts, gain, sums, output, near_inverse, near, results[4], own, halo, past1
    )
    d_own, d_halo, d_p1 = results[4:]
    back1 = lax.ppermute(d_p1, "ctx_0", [(1, 0), (2, 1), (3, 2)])
    front = lax.ppermute(d_halo, "ctx_0", [(0, 1), (1, 2), (2, 3)])
    grad_q = from_units(results[:4], info)
    totals = combine(info, d_own, back1, back2, back3, front)
    returned = [
        lax.ppermute(part, ("section", "ctx_1"), section_route(d, -1))
        for d, part in enumerate(totals)
    ]
    kv_grad = finish(info, returned).transpose(1, 0, 2)
    return normed[None], grad_q[None], kv_grad[None]


def solution(mesh):
    split = Mesh(
        mesh.devices.reshape(mesh.shape["section"], 4, 4, mesh.shape["tp"]),
        ("section", "ctx_0", "ctx_1", "tp"),
    )
    return jax.shard_map(
        whole_step,
        mesh=split,
        in_specs=(
            P("section", None, CTX, "tp"),
            P("section", CTX, None, "tp"),
            P("section", None, CTX, "tp"),
            P("section", None, "tp"),
            P(CTX),
        ),
        out_specs=(
            P("section", None, CTX, "tp"),
            P("section", None, CTX, "tp"),
            P("section", CTX, None, "tp"),
        ),
        check_vma=False,
    )
```

```python
import math

import jax
import jax.numpy as jnp
from jax import lax
from jax.experimental import pallas as pl
from jax.experimental.pallas import tpu as pltpu
from jax.sharding import Mesh
from jax.sharding import PartitionSpec as P


HD = 128
KVH = 8
GROUP = 6
FEATURES = KVH * GROUP * HD
CTX = ("ctx_0", "ctx_1")
OWN, HALO, PAST = 512, 128, 512
NEAR, FAR = OWN + HALO + PAST, 2 * PAST
SCALE = HD**-0.5
SCALE_LOG2 = SCALE * math.log2(math.e)


neg_big = -1e30
eps_norm = 1e-06
bf16 = jnp.bfloat16
f32 = jnp.float32


KEPT = pl.BlockSpec(memory_space=pltpu.VMEM)
SCALARS = pl.BlockSpec(memory_space=pltpu.SMEM)
LIMIT = pltpu.CompilerParams(vmem_limit_bytes=28 << 20)
PACKED = pltpu.CompilerParams(vmem_limit_bytes=28 << 20)


def dot_nt(a, b):
    return lax.dot_general(a, b, (((1,), (1,)), ((), ())), preferred_element_type=f32)


def dot_nn(a, b):
    return lax.dot_general(a, b, (((1,), (0,)), ((), ())), preferred_element_type=f32)


def slot(x, d):
    return pl.ds(pl.multiple_of(((x - d) & 3) * 128, 128), 128)


def at_head(head):
    return pl.ds(pl.multiple_of(head * HD, HD), HD)


def column_of(row):
    return jnp.transpose(jnp.broadcast_to(row, (128, 128)))


def order_kernel(info, a0, a1, a2, a3, own, first, turns):
    x = info[0]
    for d, ref in enumerate((a0, a1, a2, a3)):
        rows = slot(x, d)
        own[0, rows, :] = ref[0:128, :]
        own[1, rows, :] = ref[128:256, :]
        at = (x - d) & 3
        turns[pl.ds(at, 1), :] = ref[256:272, :].astype(f32)[0:1, :]

        @pl.when(at == 0)
        def _():
            first[...] = ref[...]


def put_in_order(info, parts):
    return pl.pallas_call(
        order_kernel,
        name="order_keys",
        in_specs=[SCALARS] + [KEPT] * 4,
        out_specs=[KEPT] * 3,
        out_shape=[
            pltpu.VMEM((2, 512, 128), bf16),
            pltpu.VMEM((272, 128), bf16),
            pltpu.VMEM((8, 128), f32),
        ],
        compiler_params=LIMIT,
    )(info, *parts)


def keys_of(ref, k0, n):
    return ref[k0 : k0 + n, :] if len(ref.shape) == 2 else ref[0, k0 : k0 + n, :]


def values_of(ref, k0, n):
    return ref[128 + k0 : 128 + k0 + n, :] if len(ref.shape) == 2 else ref[1, k0 : k0 + n, :]


def forward_kernel(
    info, a0, a1, a2, a3, gain_ref, turns, own, halo, p1, p2, p3,
    o_ref, l_ref, near_ref, far_ref, sums_ref, q_s, g_s, s_s, t_s, sq_s, dot_s,
):
    x, z = info[0], info[1]
    head = pl.program_id(0)
    for d, ref in enumerate((a0, a1, a2, a3)):
        q_s[slot(x, d), :] = ref[0:128, at_head(head)]
        g_s[slot(x, d), :] = ref[128:256, at_head(head)]

    @pl.when(head == 0)
    def _():
        sq_s[...] = jnp.zeros_like(sq_s)
        dot_s[...] = jnp.zeros_like(dot_s)
        for c in range(4):
            t_s[128 * c : 128 * c + 128, :] = column_of(turns[c : c + 1, :])

    halo_turns = halo[256:272, :].astype(f32)[0:1, :]

    def masked(s, b, first_key, count):
        tiles = []
        row = 256 * b + lax.broadcasted_iota(jnp.int32, (256, 128), 0)
        lane = lax.broadcasted_iota(jnp.int32, (256, 128), 1)
        mine = t_s[256 * b : 256 * b + 256, :]
        for j in range(count // 128):
            c = first_key // 128 + j
            theirs = turns[c : c + 1, :] if c < 4 else halo_turns
            seen = (lane + 128 * c <= row) | (mine == theirs)
            tiles.append(jnp.where(seen, s[:, 128 * j : 128 * j + 128], neg_big))
        return jnp.concatenate(tiles, axis=1)

    def block(b, reach):
        rows = pl.ds(256 * b, 256)
        q = q_s[rows, :]
        if b == 0:
            spans = [(own, 0, 384, near_ref, 0, True)]
        else:
            spans = [
                (own, 0, 256, near_ref, 0, False),
                (own, 256, 256, near_ref, 256, True),
                (halo, 0, 128, near_ref, OWN, True),
            ]
        if reach > 0:
            spans.append((p1, 0, 512, near_ref, OWN + HALO, False))
        if reach > 1:
            spans.append((p2, 0, 512, far_ref, 0, False))
        if reach > 2:
            spans.append((p3, 0, 512, far_ref, PAST, False))
        top = None
        for ref, k0, n, to, c0, partial in spans:
            s = dot_nt(q, keys_of(ref, k0, n))
            if partial:
                s = masked(s, b, c0, n)
            at = c0 + (NEAR if to is far_ref else 0)
            s_s[rows, at : at + n] = s
            for j in range(n // 128):
                t = s[:, 128 * j : 128 * j + 128]
                top = t if top is None else jnp.maximum(top, t)
        top = jnp.max(top, axis=1, keepdims=True) * SCALE_LOG2
        total = mixed = None
        for ref, k0, n, to, c0, _ in spans:
            at = c0 + (NEAR if to is far_ref else 0)
            e = jnp.exp2(s_s[rows, at : at + n] * SCALE_LOG2 - top)
            tiles = [e[:, 128 * j : 128 * j + 128] for j in range(n // 128)]
            while len(tiles) > 1:
                tiles = [a + c for a, c in zip(tiles[::2], tiles[1::2])] + tiles[len(tiles) & ~1 :]
            total = tiles[0] if total is None else total + tiles[0]
            e = e.astype(bf16)
            to[head, rows, c0 : c0 + n] = e
            t = dot_nn(e, values_of(ref, k0, n))
            mixed = t if mixed is None else mixed + t
        total = jnp.sum(total, axis=1, keepdims=True)
        inverse = 1.0 / total
        o = mixed * inverse
        o_ref[head, rows, :] = o
        l_ref[head, rows, :] = jnp.broadcast_to(inverse, (256, 128))
        sq_s[rows, :] += o * o
        dot_s[rows, :] += g_s[rows, :].astype(f32) * gain_ref[:, at_head(head)] * o

    for reach in range(4):

        @pl.when(z == reach)
        def _():
            block(0, reach)
            block(1, reach)

    @pl.when(head == GROUP - 1)
    def _():
        for c in range(4):
            rows = pl.ds(128 * c, 128)
            sums_ref[c : c + 1, :] = jnp.sum(jnp.transpose(sq_s[rows, :]), axis=0, keepdims=True)
            sums_ref[4 + c : 5 + c, :] = jnp.sum(
                jnp.transpose(dot_s[rows, :]), axis=0, keepdims=True
            )


def forward(info, parts, gain, turns, own, halo, past):
    return pl.pallas_call(
        forward_kernel,
        name="attention_forward",
        grid_spec=pltpu.PrefetchScalarGridSpec(
            num_scalar_prefetch=1,
            grid=(GROUP,),
            in_specs=[KEPT] * 11,
            out_specs=[KEPT] * 5,
            scratch_shapes=[
                pltpu.VMEM((512, 128), bf16),
                pltpu.VMEM((512, 128), bf16),
                pltpu.VMEM((512, NEAR + FAR), f32),
                pltpu.VMEM((512, 128), f32),
                pltpu.VMEM((512, 128), f32),
                pltpu.VMEM((512, 128), f32),
            ],
        ),
        out_shape=[
            pltpu.VMEM((GROUP, 512, HD), f32),
            pltpu.VMEM((GROUP, 512, HD), f32),
            pltpu.VMEM((GROUP, 512, NEAR), bf16),
            pltpu.VMEM((GROUP, 512, FAR), bf16),
            pltpu.VMEM((8, 128), f32),
        ],
        compiler_params=PACKED,
    )(info, *parts, gain, turns, own, halo, *past)


def cotangent_rows(q_s, g_s, gain_ref, r_s, c_s, o_ref, l_ref):
    output = o_ref[pl.program_id(0)]
    scaled = g_s[...].astype(f32) * gain_ref[:, at_head(pl.program_id(0))]
    grad = (r_s[...] * (scaled - output * c_s[...]) * l_ref[pl.program_id(0)]).astype(bf16)
    wide = grad.astype(f32)
    row_dot = jnp.sum(wide * output, axis=1, keepdims=True)
    grad_t = jnp.transpose(grad)
    query_t = jnp.transpose(q_s[...])
    return grad, row_dot, grad_t, query_t


def fill_columns(sums, r_s, c_s):
    for c in range(4):
        inverse = lax.rsqrt(sums[c : c + 1, :] / FEATURES + eps_norm)
        center = sums[4 + c : 5 + c, :] / FEATURES
        r_s[128 * c : 128 * c + 128, :] = column_of(inverse)
        c_s[128 * c : 128 * c + 128, :] = column_of(inverse * inverse * center)


def spans_back(spans, e_ref, rows_of, grad_q, dk_s, dv_s):
    grad, row_dot, grad_t, query_t = rows_of
    for ref, k0, n, c0, r0, count in spans:
        e = e_ref[pl.program_id(0), r0 : r0 + count, c0 : c0 + n]
        grad_p = dot_nt(grad[r0 : r0 + count, :], values_of(ref, k0, n))
        grad_s = (e.astype(f32) * (grad_p - row_dot[r0 : r0 + count, :])).astype(bf16)
        t = dot_nn(grad_s, keys_of(ref, k0, n))
        for b in range(count // 256):
            i = r0 // 256 + b
            part = t[256 * b : 256 * b + 256]
            grad_q[i] = part if grad_q[i] is None else grad_q[i] + part
        dv_s[:, c0 : c0 + n] += dot_nn(grad_t[:, r0 : r0 + count], e)
        dk_s[:, c0 : c0 + n] += dot_nn(query_t[:, r0 : r0 + count], grad_s)


def write_keys(refs, starts, dk_s, dv_s):
    for ref, c0 in zip(refs, starts):
        n = ref.shape[2]
        ref[0] = (dk_s[:, c0 : c0 + n] * SCALE).astype(ref.dtype)
        ref[1] = dv_s[:, c0 : c0 + n].astype(ref.dtype)


def far_kernel(
    info, a0, a1, a2, a3, gain_ref, sums, o_ref, l_ref, e_ref, p2, p3,
    n0, n1, n2, n3, dq_ref, d_p2, d_p3, q_s, g_s, dk_s, dv_s, r_s, c_s,
):
    x, z = info[0], info[1]
    head = pl.program_id(0)

    @pl.when(head == 0)
    def _():
        dk_s[...] = jnp.zeros_like(dk_s)
        dv_s[...] = jnp.zeros_like(dv_s)
        fill_columns(sums, r_s, c_s)

    for d, ref in enumerate((n0, n1, n2, n3)):
        rows = slot(x, d)
        ref[:, at_head(head)] = (
            o_ref[head, rows, :] * r_s[rows, :] * gain_ref[:, at_head(head)]
        ).astype(bf16)

    @pl.when(z < 2)
    def _():
        dq_ref[head] = jnp.zeros((512, HD), f32)

    for reach in (2, 3):

        @pl.when(z == reach)
        def _():
            for d, ref in enumerate((a0, a1, a2, a3)):
                q_s[slot(x, d), :] = ref[0:128, at_head(head)]
                g_s[slot(x, d), :] = ref[128:256, at_head(head)]
            rows_of = cotangent_rows(q_s, g_s, gain_ref, r_s, c_s, o_ref, l_ref)
            spans = [(p2, 0, 512, 0, 0, 512), (p3, 0, 512, PAST, 0, 512)][: reach - 1]
            grad_q = [None, None]
            spans_back(spans, e_ref, rows_of, grad_q, dk_s, dv_s)
            dq_ref[head] = jnp.concatenate(grad_q, axis=0)

    @pl.when((head == GROUP - 1) & (z > 1))
    def _():
        write_keys((d_p2, d_p3), (0, PAST), dk_s, dv_s)


def backward_far(info, parts, gain, sums, output, totals, weights, p2, p3):
    return pl.pallas_call(
        far_kernel,
        name="backward_far",
        grid_spec=pltpu.PrefetchScalarGridSpec(
            num_scalar_prefetch=1,
            grid=(GROUP,),
            in_specs=[KEPT] * 11,
            out_specs=[KEPT] * 7,
            scratch_shapes=[pltpu.VMEM((512, 128), bf16)] * 2
            + [pltpu.VMEM((128, FAR), f32)] * 2
            + [pltpu.VMEM((512, 128), f32)] * 2,
        ),
        out_shape=[pltpu.VMEM((128, GROUP * HD), bf16)] * 4
        + [pltpu.VMEM((GROUP, 512, HD), f32)]
        + [pltpu.VMEM((2, 128, 512), bf16)] * 2,
        compiler_params=PACKED,
    )(info, *parts, gain, sums, output, totals, weights, p2, p3)


def near_kernel(
    info, a0, a1, a2, a3, gain_ref, sums, o_ref, l_ref, e_ref, dq_ref,
    own, halo, p1,
    dq0, dq1, dq2, dq3, d_own, d_halo, d_p1, q_s, g_s, dq_s, dk_s, dv_s, r_s, c_s,
):
    x, z = info[0], info[1]
    head = pl.program_id(0)
    for d, ref in enumerate((a0, a1, a2, a3)):
        q_s[slot(x, d), :] = ref[0:128, at_head(head)]
        g_s[slot(x, d), :] = ref[128:256, at_head(head)]

    @pl.when(head == 0)
    def _():
        dk_s[...] = jnp.zeros_like(dk_s)
        dv_s[...] = jnp.zeros_like(dv_s)
        fill_columns(sums, r_s, c_s)

    rows_of = cotangent_rows(q_s, g_s, gain_ref, r_s, c_s, o_ref, l_ref)

    def body(reach):
        spans = [
            (own, 0, 384, 0, 0, 256),
            (own, 0, 512, 0, 256, 256),
            (halo, 0, 128, OWN, 256, 256),
        ]
        if reach:
            spans.append((p1, 0, 512, OWN + HALO, 0, 512))
        grad_q = [dq_ref[head, 0:256, :], dq_ref[head, 256:512, :]]
        spans_back(spans, e_ref, rows_of, grad_q, dk_s, dv_s)
        dq_s[...] = (jnp.concatenate(grad_q, axis=0) * SCALE).astype(bf16)

    @pl.when(z == 0)
    def _():
        body(0)

    @pl.when(z > 0)
    def _():
        body(1)

    for d, ref in enumerate((dq0, dq1, dq2, dq3)):
        ref[:, at_head(head)] = dq_s[slot(x, d), :]

    @pl.when(head == GROUP - 1)
    def _():
        write_keys((d_own, d_halo, d_p1), (0, OWN, OWN + HALO), dk_s, dv_s)


def backward_near(info, parts, gain, sums, output, totals, weights, dq, own, halo, p1):
    return pl.pallas_call(
        near_kernel,
        name="backward_near",
        grid_spec=pltpu.PrefetchScalarGridSpec(
            num_scalar_prefetch=1,
            grid=(GROUP,),
            in_specs=[KEPT] * 13,
            out_specs=[KEPT] * 7,
            scratch_shapes=[pltpu.VMEM((512, 128), bf16)] * 3
            + [pltpu.VMEM((128, NEAR), f32)] * 2
            + [pltpu.VMEM((512, 128), f32)] * 2,
        ),
        out_shape=[pltpu.VMEM((128, GROUP * HD), bf16)] * 4
        + [
            pltpu.VMEM((2, 128, 512), f32),
            pltpu.VMEM((2, 128, 128), bf16),
            pltpu.VMEM((2, 128, 512), bf16),
        ],
        compiler_params=LIMIT,
    )(info, *parts, gain, sums, output, totals, weights, dq, own, halo, p1)


def combine_kernel(info, own, back1, back2, back3, front, r0, r1, r2, r3, total):
    x = info[0]
    for c in range(4):
        at = pl.ds(128 * c, 128)
        part = own[:, :, at] + back1[:, :, at].astype(f32)
        part = part + back2[:, :, at].astype(f32) + back3[:, :, at].astype(f32)
        if c == 0:
            part = part + front[...].astype(f32)
        total[c] = part.astype(bf16)
    for d, ref in enumerate((r0, r1, r2, r3)):
        ref[...] = total[(x - d) & 3]


def combine(info, own, back1, back2, back3, front):
    return pl.pallas_call(
        combine_kernel,
        name="combine",
        in_specs=[SCALARS] + [KEPT] * 5,
        out_specs=[KEPT] * 4,
        out_shape=[pltpu.VMEM((2, 128, 128), bf16)] * 4,
        scratch_shapes=[pltpu.VMEM((4, 2, 128, 128), bf16)],
        compiler_params=LIMIT,
    )(info, own, back1, back2, back3, front)


def finish_kernel(info, r0, r1, r2, r3, out):
    x = info[0]
    for a, b, flip in ((r0, r2, 0), (r1, r3, 1)):
        at = pl.ds(pl.multiple_of(((x + flip) & 1) * 128, 128), 128)
        for half in range(2):
            both = a[half].astype(f32) + b[half].astype(f32)
            out[half, :, at] = jnp.transpose(both)


def finish(info, parts):
    return pl.pallas_call(
        finish_kernel,
        name="finish",
        in_specs=[SCALARS] + [KEPT] * 4,
        out_specs=KEPT,
        out_shape=pltpu.VMEM((2, 128, 256), f32),
        compiler_params=LIMIT,
    )(info, *parts)


def gather_kernel(info, r0, r1, r2, r3, out):
    x = info[0]
    for d, ref in enumerate((r0, r1, r2, r3)):
        unit = (x + d) & 3
        at = pl.ds(pl.multiple_of((unit & 1) * GROUP * HD, 128), GROUP * HD)
        out[unit >> 1, :, at] = ref[...]


def gather(info, parts):
    return pl.pallas_call(
        gather_kernel,
        name="gather",
        in_specs=[SCALARS] + [KEPT] * 4,
        out_specs=KEPT,
        out_shape=jax.ShapeDtypeStruct((2, 128, 2 * GROUP * HD), bf16),
        compiler_params=LIMIT,
    )(info, *parts)


def along(x, axis, pairs):
    return lax.ppermute(x, axis, pairs)


def unit_of(block, unit):
    return lax.dynamic_slice(
        block, (unit // 2, 0, (unit % 2) * GROUP * HD), (1, 128, GROUP * HD)
    )[0]


def to_units(first, second, x):
    parts = []
    for d in range(4):
        unit = (x + d) & 3
        part = jnp.concatenate([unit_of(first, unit), unit_of(second, unit)], axis=0)
        parts.append(
            part if d == 0 else along(part, "ctx_1", [(i, (i + d) % 4) for i in range(4)])
        )
    return parts


def from_units(parts, info):
    got = [parts[0]]
    for d in range(1, 4):
        got.append(along(parts[d], "ctx_1", [(i, (i - d) % 4) for i in range(4)]))
    return gather(info, got)


def section_route(d, sign):
    route = []
    for s in range(4):
        for i in range(4):
            if sign > 0:
                unit = (i + d) % 4
                route.append((s * 4 + i, (s + unit // 2) % 4 * 4 + unit))
            else:
                route.append((s * 4 + i, (s - i // 2) % 4 * 4 + (i - d) % 4))
    return route


def whole_step(query_heads, keys_values, grad_output, norm_gain, turn_ids):
    z = lax.axis_index("ctx_0")
    x = lax.axis_index("ctx_1")
    info = jnp.stack([x, z]).astype(jnp.int32)

    turn_rows = jnp.broadcast_to(turn_ids.astype(bf16)[None], (16, 128))
    kv = keys_values[0]
    heads = [
        jnp.concatenate([kv[:, 0, a : a + HD], kv[:, 1, a : a + HD], turn_rows], axis=0)
        for a in (0, HD)
    ]
    odd = (x & 1) == 1
    same = jnp.where(odd, heads[1], heads[0])
    other = jnp.where(odd, heads[0], heads[1])
    received = [
        along(same if d % 2 == 0 else other, ("section", "ctx_1"), section_route(d, 1))
        for d in range(4)
    ]
    parts = to_units(query_heads[0], grad_output[0], x)
    own, first, turns = put_in_order(info, received)
    halo = along(first, "ctx_0", [(1, 0), (2, 1), (3, 2)])
    past2 = along(own, "ctx_0", [(0, 2), (1, 3)])
    past1 = along(own, "ctx_0", [(0, 1), (1, 2), (2, 3)])
    past3 = along(past2, "ctx_0", [(2, 3)])
    gain = lax.dynamic_slice(norm_gain[0], (x // 2, (x % 2) * GROUP * HD), (1, GROUP * HD))

    output, totals, near, far, sums = forward(
        info, parts, gain, turns, own, halo, (past1, past2, past3)
    )
    sums = sums + along(sums, "tp", [(i, i ^ 1) for i in range(4)])
    sums = sums + along(sums, "ctx_1", [(i, i ^ 1) for i in range(4)])
    sums = sums + along(sums, "tp", [(i, i ^ 2) for i in range(4)])

    results = backward_far(info, parts, gain, sums, output, totals, far, past2, past3)
    d_p2, d_p3 = results[5:]
    back3 = along(d_p3, "ctx_0", [(3, 0)])
    back2 = along(d_p2, "ctx_0", [(2, 0), (3, 1)])
    normed = from_units(results[:4], info)
    results = backward_near(
        info, parts, gain, sums, output, totals, near, results[4], own, halo, past1
    )
    d_own, d_halo, d_p1 = results[4:]
    back1 = along(d_p1, "ctx_0", [(1, 0), (2, 1), (3, 2)])
    front = along(d_halo, "ctx_0", [(0, 1), (1, 2), (2, 3)])
    grad_q = from_units(results[:4], info)
    totals = combine(info, d_own, back1, back2, back3, front)
    returned = [
        along(part, ("section", "ctx_1"), section_route(d, -1))
        for d, part in enumerate(totals)
    ]
    kv_grad = finish(info, returned).transpose(1, 0, 2)
    return normed[None], grad_q[None], kv_grad[None]


def solution(mesh):
    split = Mesh(
        mesh.devices.reshape(mesh.shape["section"], 4, 4, mesh.shape["tp"]),
        ("section", "ctx_0", "ctx_1", "tp"),
    )
    return jax.shard_map(
        whole_step,
        mesh=split,
        in_specs=(
            P("section", None, CTX, "tp"),
            P("section", CTX, None, "tp"),
            P("section", None, CTX, "tp"),
            P("section", None, "tp"),
            P(CTX),
        ),
        out_specs=(
            P("section", None, CTX, "tp"),
            P("section", None, CTX, "tp"),
            P("section", CTX, None, "tp"),
        ),
        check_vma=False,
    )
```
